256 devices in a mesh: cam: 8 (over x, core), clip: 32 (over y, z).
Axes of the slice: x: 4, y: 4, z: 8, core: 2. Of those that a mesh axis runs over, the one named last changes fastest.
Arguments:
- tokens: bfloat16 [64, 8, 256, 1024], P('clip', 'cam'), may hold values from -6 to 6
- w_query: bfloat16 [1024, 1024], replicated, may hold values from -0.1875 to 0.1875
- w_key: bfloat16 [1024, 1024], replicated, may hold values from -0.1875 to 0.1875
- w_value: bfloat16 [1024, 1024], replicated, may hold values from -0.1875 to 0.1875
- w_proj: bfloat16 [1024, 256], replicated, may hold values from -0.1875 to 0.1875
- prototypes: bfloat16 [256, 65536], P(None, ('cam', 'clip')), may hold values from -6 to 6
Outputs:
- codes: float32 [64, 65536], P(None, ('cam', 'clip'))
- prototype_gradient: float32 [256, 65536], P(None, ('cam', 'clip'))
- grad_proj: float32 [1024, 256], P('clip')
- grad_value: float32 [1024, 1024], P('clip', 'cam')
The draws below stay inside these ranges and needn't reach their ends.
All inputs are finite; a program needn't handle non-finite values.
Results may differ from the reference program's by a relative error of at most 0.015.
Values may be sent and summed in bfloat16 or wider, within the bound.
A program may use at most 128 MiB of HBM per device.

```python
import jax
import jax.numpy as jnp
from jax import lax

D = 1024
HD = 64
BOT = 256
PROTOS = 65536
TOK = 256
ITERS = 3
H = 16
CAMS = 8
CLIPS = 64
N_CAM = 8


def draw_prototypes(key, part):
    groups = 16
    key_dirs, key_noise, key_member, key_sign, key_scale = jax.random.split(jax.random.fold_in(key, 7), 5)
    directions = jnp.clip(jax.random.normal(key_dirs, (BOT, groups), jnp.float32), -4.0, 4.0)
    noise = 0.5 * jnp.clip(jax.random.normal(key_noise, (BOT, PROTOS), jnp.float32), -4.0, 4.0)
    members = jax.random.randint(key_member, (PROTOS,), 0, groups)
    signs = 2.0 * jax.random.randint(key_sign, (PROTOS,), 0, 2).astype(jnp.float32) - 1.0
    scales = jax.random.uniform(key_scale, (PROTOS,), jnp.float32, 0.5, 1.0)
    picked = jnp.take(directions, members, axis=1)
    values = (picked * signs[None, :] + noise) * scales[None, :]
    return values.astype(jnp.bfloat16)


def level_of(stream_key, extent, shards, least, largest):
    gain = 1.0
    for axis_at, shards_of in shards:
        heights = jax.random.uniform(jax.random.fold_in(jax.random.fold_in(stream_key, 6), axis_at), (shards_of,), jnp.float32, least / len(shards), largest / len(shards))
        gain = gain * jnp.repeat(jnp.exp(heights), extent[axis_at] // shards_of).reshape((-1,) + (1,) * (len(extent) - 1 - axis_at))
    return gain


def normal_values(key, shape, spread, most, cuts=(), kind=jnp.bfloat16):
    entries = spread * jax.random.normal(key, shape, jnp.float32)
    if cuts:
        entries = entries * level_of(key, shape, cuts, -0.22, 0.18)
    return jnp.clip(entries, -most, most).astype(kind)


def setup_inputs(seed: int = 0) -> dict:
    splits = jax.random.split(jax.random.key(seed), 7)
    return {
        "tokens": normal_values(splits[0], (CLIPS, CAMS, TOK, D), 1.0, 6.0, ((0, 32), (1, 8))),
        "w_query": normal_values(splits[1], (D, D), D ** -0.5, 0.1875),
        "w_key": normal_values(splits[2], (D, D), D ** -0.5, 0.1875),
        "w_value": normal_values(splits[3], (D, D), D ** -0.5, 0.1875),
        "w_proj": normal_values(splits[4], (D, BOT), D ** -0.5, 0.1875),
        "prototypes": draw_prototypes(jax.random.fold_in(splits[6], 71), 0),
    }


SINK_EPS = 0.05
SOFTMAX_TEMP = 0.1
NORM_EPS = 1e-06

def column_averages(query_vectors, key_rows):
    total = key_rows.shape[0]

    def per_head(index):
        query_head = lax.dynamic_slice_in_dim(query_vectors, index * HD, HD, 1).astype(jnp.float32)
        key_head = lax.dynamic_slice_in_dim(key_rows, index * HD, HD, 1).astype(jnp.float32)
        scores = jnp.dot(query_head, key_head.T, precision=lax.Precision.HIGHEST) * HD ** (-0.5)
        exponent_values = jnp.exp(scores)
        probs = exponent_values / lax.optimization_barrier(jnp.sum(exponent_values, axis=1, keepdims=True))
        return lax.optimization_barrier(jnp.sum(probs, axis=0)) / total
    return lax.map(per_head, jnp.arange(H, dtype=jnp.int32))

def reference(tokens, w_query, w_key, w_value, w_proj, prototypes):
    value_heads = w_value.astype(jnp.float32).reshape(D, H, HD)

    def pool_clip(clip_rows):
        flat = clip_rows.reshape(N_CAM * TOK, D)
        query_vectors = jnp.dot(flat, w_query, preferred_element_type=jnp.float32).astype(jnp.bfloat16)
        key_rows = jnp.dot(flat, w_key, preferred_element_type=jnp.float32).astype(jnp.bfloat16)
        weights = column_averages(query_vectors, key_rows).astype(jnp.bfloat16).reshape(H, N_CAM, TOK)
        mixture = jnp.einsum('hcj,cjd->chd', weights.astype(jnp.float32), clip_rows.astype(jnp.float32), precision=lax.Precision.HIGHEST).astype(jnp.bfloat16)
        head_out = jnp.einsum('chd,dhe->che', mixture.astype(jnp.float32), value_heads, precision=lax.Precision.HIGHEST)
        return (lax.optimization_barrier(jnp.sum(head_out, axis=0)).reshape(D).astype(jnp.bfloat16), mixture)
    pooled, mixtures = lax.map(pool_clip, tokens)
    embed = jnp.dot(pooled, w_proj, preferred_element_type=jnp.float32)
    embed_norm = jnp.sqrt(lax.optimization_barrier(jnp.sum(embed * embed, axis=1, keepdims=True)) + NORM_EPS)
    unit = embed / embed_norm
    unit_b = unit.astype(jnp.bfloat16)
    proto_f = prototypes.astype(jnp.float32)
    column_norm = jnp.sqrt(lax.optimization_barrier(jnp.sum(proto_f * proto_f, axis=0, keepdims=True)) + NORM_EPS)
    unit_proto = proto_f / column_norm
    proto_b = unit_proto.astype(jnp.bfloat16)
    logit_scores = jnp.dot(unit_b, proto_b, preferred_element_type=jnp.float32)
    assign = jnp.exp(logit_scores / SINK_EPS)
    for step in range(ITERS):
        assign = assign / lax.optimization_barrier(jnp.sum(assign, axis=0, keepdims=True))
        assign = assign / lax.optimization_barrier(jnp.sum(assign, axis=1, keepdims=True))
    exponent_values = jnp.exp(logit_scores / SOFTMAX_TEMP)
    prob = exponent_values / lax.optimization_barrier(jnp.sum(exponent_values, axis=1, keepdims=True))
    grad_logits = (PROTOS * (prob - assign)).astype(jnp.bfloat16)
    codes = PROTOS * assign
    grad_unit = jnp.dot(grad_logits, proto_b.T, preferred_element_type=jnp.float32)
    grad_embed = (grad_unit - unit * lax.optimization_barrier(jnp.sum(unit * grad_unit, axis=1, keepdims=True))) / embed_norm
    grad_embed_b = grad_embed.astype(jnp.bfloat16)
    grad_proj = jnp.dot(pooled.T, grad_embed_b, preferred_element_type=jnp.float32)
    grad_pooled = jnp.dot(grad_embed_b, w_proj.T, preferred_element_type=jnp.float32).astype(jnp.bfloat16)
    grad_value = jnp.einsum('bchd,bhe->dhe', mixtures.astype(jnp.float32), grad_pooled.astype(jnp.float32).reshape(CLIPS, H, HD), precision=lax.Precision.HIGHEST).reshape(D, D)
    grad_unit_proto = jnp.dot(unit_b.T, grad_logits, preferred_element_type=jnp.float32)
    prototype_gradient = (grad_unit_proto - unit_proto * lax.optimization_barrier(jnp.sum(unit_proto * grad_unit_proto, axis=0, keepdims=True))) / column_norm
    return (codes, prototype_gradient, grad_proj, grad_value)
```

```python
import functools

import jax
import jax.numpy as jnp
from jax import lax
from jax.experimental import pallas as pl
from jax.experimental.pallas import tpu as pltpu
from jax.sharding import PartitionSpec as P

D = 1024
HD = 64
H = 16
BOT = 256
PROTOS = 65536
TOK = 256
CLIPS = 64
N_CAM = 8
N_CLIP = 32
N_Z = 8
N_Y = N_CLIP // N_Z
N_R = N_CAM * N_Y
PAIR = 2
LANES = 128
COLS = PROTOS // (N_CAM * N_CLIP)
SHARE = D // N_CLIP
KEYS = N_CAM * TOK
ROWS_AT_ONCE = 1024

SINK_EPS = 0.05
SOFTMAX_TEMP = 0.1
NORM_EPS = 1e-06
LOG2_E = 1.4426950408889634

MESH = pl.DeviceIdType.MESH
F32 = jnp.float32
BF16 = jnp.bfloat16


def dot(a, b, dims):
    return lax.dot_general(a, b, (dims, ((), ())), preferred_element_type=F32)


NN = ((1,), (0,))
NT = ((1,), (1,))
TN = ((0,), (0,))


def fold(a):
    return a[:, :LANES] + a[:, LANES:]


def twice(a):
    return jnp.concatenate([a, a], axis=1)


def kernel(
    x_in, wq_in, wk_in, wv_in, wp_in, pr_in,
    codes_out, proto_out, proj_out, value_out,
    xv, wq, wk, wv, wp, pr,
    proto_all, qk_send, qk_recv, acc,
    w_send, w_recv, mix_send, mix_recv, pool_send, pool_recv,
    z_send, z_recv, side_send, side_recv,
    a_buf, p_buf, v_buf, g_buf, unit_buf, norm_buf,
    row_send, row_recv, gu_send, gu_recv, gz_send, gz_recv,
    proj_tmp, value_tmp,
    load_sem, own_sem, qk_ss, qk_rs, cam_ss, cam_rs, proto_ss, proto_rs, wide_ss, wide_rs,
):
    cam = lax.axis_index("cam")
    clip = lax.axis_index("clip")
    y, z = lax.div(clip, N_Z), lax.rem(clip, N_Z)
    here = y * N_CAM + cam

    loads = [
        pltpu.make_async_copy(x_in, xv, load_sem.at[0]),
        pltpu.make_async_copy(wq_in, wq, load_sem.at[1]),
        pltpu.make_async_copy(wk_in, wk, load_sem.at[2]),
        pltpu.make_async_copy(pr_in, pr, load_sem.at[3]),
        pltpu.make_async_copy(wv_in, wv, load_sem.at[4]),
        pltpu.make_async_copy(wp_in, wp, load_sem.at[5]),
    ]
    for load in loads:
        load.start()

    def cam_peer(o):
        return (lax.rem(cam + o, N_CAM), clip)

    def clip_peer(o):
        return (cam, lax.rem(clip + o, N_CLIP))

    def z_peer(o):
        return (cam, y * N_Z + lax.rem(z + o, N_Z))

    def r_peer(o):
        other = lax.rem(here + o, N_R)
        return (lax.rem(other, N_CAM), lax.div(other, N_CAM) * N_Z + z)

    def loop(lo, hi, step):
        def body(i, carry):
            step(i)
            return carry

        lax.fori_loop(lo, hi, body, 0)

    barrier = pltpu.get_barrier_semaphore()

    def greet(device):
        pl.semaphore_signal(barrier, inc=1, device_id=device, device_id_type=MESH)

    loop(1, N_CAM, lambda o: greet(cam_peer(o)))
    loop(1, N_CLIP, lambda o: greet(clip_peer(o)))

    def greet_rest(i):
        oc, oy = 1 + lax.div(i, N_Y - 1), 1 + lax.rem(i, N_Y - 1)
        greet((lax.rem(cam + oc, N_CAM), lax.rem(y + oy, N_Y) * N_Z + z))

    rest = (N_CAM - 1) * (N_Y - 1)
    loop(0, rest, greet_rest)

    def project(b):
        rows = xv[b * TOK : (b + 1) * TOK, :]
        for which, weight in enumerate((wq, wk)):
            for j in range(D // 256):
                got = dot(rows, weight[:, j * 256 : (j + 1) * 256], NN).astype(BF16)
                qk_send[b, 2 * j, which] = got[:, :LANES]
                qk_send[b, 2 * j + 1, which] = got[:, LANES:]

    def qk_copy(b, o):
        to = cam_peer(o)
        return pltpu.make_async_remote_copy(
            src_ref=qk_send.at[b, to[0]], dst_ref=qk_recv.at[b, cam],
            send_sem=qk_ss.at[b, o], recv_sem=qk_rs.at[b, o],
            device_id=to, device_id_type=MESH,
        )

    def own_copy(b):
        return pltpu.make_async_copy(qk_send.at[b, cam], qk_recv.at[b, cam], own_sem.at[b])

    def proto_copy(o):
        return pltpu.make_async_remote_copy(
            src_ref=proto_all.at[z], dst_ref=proto_all.at[z],
            send_sem=proto_ss.at[o], recv_sem=proto_rs.at[o],
            device_id=z_peer(o), device_id_type=MESH,
        )

    for load in loads[:3]:
        load.wait()
    project(0)
    pl.semaphore_wait(barrier, N_CAM - 1 + N_CLIP - 1 + rest)
    loop(1, N_CAM, lambda o: qk_copy(0, o).start())
    own_copy(0).start()
    project(1)
    loop(1, N_CAM, lambda o: qk_copy(1, o).start())
    own_copy(1).start()

    loads[3].wait()
    proto = pr[...].astype(F32)
    col_norm = jnp.sqrt(jnp.sum(proto * proto, axis=0, keepdims=True) + NORM_EPS)
    proto_all[z] = (proto / col_norm).astype(BF16)
    loop(1, N_Z, lambda o: proto_copy(o).start())

    acc[...] = jnp.zeros_like(acc)
    cams_at_once = ROWS_AT_ONCE // TOK
    lane_q = lax.broadcasted_iota(jnp.int32, (ROWS_AT_ONCE, LANES), 1)

    def attend(b):
        loop(1, N_CAM, lambda o: qk_copy(b, o).wait_recv())
        own_copy(b).wait()

        def block(i):
            head, part = lax.div(i, N_CAM // cams_at_once), lax.rem(i, N_CAM // cams_at_once)
            keys = qk_recv[b, :, 1].reshape(KEYS, LANES)
            rows = qk_recv[b, pl.ds(part * cams_at_once, cams_at_once), 0].reshape(ROWS_AT_ONCE, LANES)
            rows = jnp.where(lax.div(lane_q, HD) == head, rows, jnp.zeros_like(rows))
            weights = jnp.exp2(dot(rows, keys, NT) * (HD ** (-0.5) * LOG2_E))
            weights = weights * (1.0 / jnp.sum(weights, axis=1, keepdims=True))
            acc[b * PAIR + head] += jnp.sum(weights.reshape(ROWS_AT_ONCE // 8, 8, KEYS), axis=0)

        loop(0, PAIR * N_CAM // cams_at_once, block)

    loop(0, PAIR, attend)

    def cam_copy(k, src, dst, o):
        to = cam_peer(o)
        return pltpu.make_async_remote_copy(
            src_ref=src(to[0]), dst_ref=dst, send_sem=cam_ss.at[k, o], recv_sem=cam_rs.at[k, o],
            device_id=to, device_id_type=MESH,
        )

    def wide_copy(k, src, dst, peer, o):
        to = peer(o)
        return pltpu.make_async_remote_copy(
            src_ref=src(to), dst_ref=dst, send_sem=wide_ss.at[k, o], recv_sem=wide_rs.at[k, o],
            device_id=to, device_id_type=MESH,
        )

    def w_copy(o):
        return cam_copy(0, lambda p: w_send.at[p], w_recv.at[cam], o)

    def pool_copy(o):
        return cam_copy(1, lambda p: pool_send, pool_recv.at[cam], o)

    def mix_copy(o):
        return cam_copy(2, lambda p: mix_send.at[p], mix_recv.at[cam], o)

    def gz_copy(o):
        return cam_copy(3, lambda p: gz_send, gz_recv.at[cam], o)

    def z_copy(o):
        return wide_copy(0, lambda to: z_send, z_recv.at[clip], clip_peer, o)

    def side_copy(o):
        return wide_copy(
            1, lambda to: side_send.at[lax.div(to[1] * SHARE, LANES)], side_recv.at[clip], clip_peer, o
        )

    def gu_copy(o):
        return wide_copy(2, lambda to: gu_send.at[to[0]], gu_recv.at[here], r_peer, o)

    def row_copy(step, o):
        return wide_copy(3 + step, lambda to: row_send.at[step], row_recv.at[step, here], r_peer, o)

    row8 = lax.broadcasted_iota(jnp.int32, (8, KEYS), 0)
    weights = jnp.zeros((8, KEYS), F32)
    for r in range(PAIR * PAIR):
        weights = jnp.where(row8 == r, jnp.sum(acc[r], axis=0, keepdims=True) * (1.0 / KEYS), weights)
    for p in range(N_CAM):
        w_send[p] = weights[:, p * TOK : (p + 1) * TOK]
    loop(1, N_CAM, lambda o: w_copy(o).start())
    w_recv[cam] = w_send[cam]
    loads[4].wait()
    loop(1, N_CAM, lambda o: w_copy(o).wait_recv())

    key_weight = w_recv[...].reshape(8 * N_CAM, TOK).astype(BF16)
    mix0 = dot(key_weight, xv[:TOK, :], NN)
    mix1 = dot(key_weight, xv[TOK:, :], NN)
    row64 = lax.broadcasted_iota(jnp.int32, (8 * N_CAM, D), 0)
    mixture = jnp.where(lax.rem(row64, 8) >= PAIR, mix1, mix0).astype(BF16)
    head_out = dot(mixture, wv[...], NN)
    lane8 = lax.broadcasted_iota(jnp.int32, (8, LANES), 1)
    sub8 = lax.broadcasted_iota(jnp.int32, (8, LANES), 0)
    own_head = lax.rem(sub8, PAIR) == lax.div(lane8, HD)
    for p in range(N_CAM):
        tile = head_out[p * 8 : (p + 1) * 8, p * LANES : (p + 1) * LANES]
        tile = jnp.where(own_head, tile, 0.0)
        pool_send[p : p + 1, :] = tile[0:1] + tile[1:2]
        pool_send[N_CAM + p : N_CAM + p + 1, :] = tile[2:3] + tile[3:4]
    loop(1, N_CAM, lambda o: pool_copy(o).start())
    pool_recv[cam] = pool_send[...]
    mixture_f = mixture.astype(F32)
    for p in range(N_CAM):
        mix_send[p] = mixture_f[p * 8 : p * 8 + PAIR * PAIR, :]
    loop(1, N_CAM, lambda o: mix_copy(o).start())
    mix_recv[cam] = mix_send[cam]
    loads[5].wait()
    loop(1, N_CAM, lambda o: pool_copy(o).wait_recv())
    pooled = jnp.sum(pool_recv[...], axis=0).astype(BF16)
    row16 = lax.broadcasted_iota(jnp.int32, (PAIR * N_CAM, LANES), 0)
    spread = jnp.concatenate(
        [jnp.where(lax.rem(row16, N_CAM) == p, pooled, jnp.zeros_like(pooled)) for p in range(N_CAM)], axis=1
    )
    z_rows = dot(spread, wp[...], NN)
    for b in range(PAIR):
        z_clip = jnp.sum(z_rows[b * N_CAM : (b + 1) * N_CAM], axis=0, keepdims=True)
        for j in range(2):
            z_send[2 * b + j : 2 * b + j + 1, :] = z_clip[:, j * LANES : (j + 1) * LANES]
    loop(1, N_CLIP, lambda o: z_copy(o).start())
    z_recv[clip] = z_send[...]

    loop(1, N_CAM, lambda o: mix_copy(o).wait_recv())
    mix_sum = jnp.sum(mix_recv[...], axis=0)
    pooled_f = pooled.astype(F32)
    for p in range(N_CAM):
        side_send[p, 0:1, :] = pooled_f[p : p + 1]
        side_send[p, 1:2, :] = pooled_f[N_CAM + p : N_CAM + p + 1]
        side_send[p, 2:6, :] = mix_sum[:, p * LANES : (p + 1) * LANES]
        side_send[p, 6:8, :] = jnp.zeros((2, LANES), F32)
    loop(1, N_Z, lambda o: proto_copy(o).wait_recv())
    loop(1, N_CLIP, lambda o: z_copy(o).wait_recv())
    loop(1, N_CLIP, lambda o: side_copy(o).start())
    side_recv[clip] = side_send[lax.div(clip * SHARE, LANES)]

    embed = jnp.concatenate(
        [jnp.concatenate([z_recv[:, 2 * b + j, :] for j in range(2)], axis=1) for b in range(PAIR)], axis=0
    )
    norm = jnp.sqrt(jnp.sum(embed * embed, axis=1, keepdims=True) + NORM_EPS)
    unit = embed / norm
    unit_buf[...] = unit
    norm_buf[...] = jnp.broadcast_to(norm, norm_buf.shape)
    unit_b = unit.astype(BF16)

    def total(step, sums):
        tall = jnp.broadcast_to(jnp.sum(sums, axis=1, keepdims=True), (LANES, LANES))
        row_send[step] = tall.T[:8, :]
        loop(1, N_R, lambda o: row_copy(step, o).start())
        row_recv[step, here] = row_send[step]
        loop(1, N_R, lambda o: row_copy(step, o).wait_recv())
        wide = jnp.sum(row_recv[step], axis=0)
        return jnp.broadcast_to(wide[0:1], (LANES, LANES)).T

    zero = jnp.zeros((CLIPS, LANES), F32)

    def first(s, carry):
        rows, probs = carry
        exps = jnp.exp(dot(unit_b, proto_all[s], NN) * (1.0 / SOFTMAX_TEMP))
        scores = exps * exps
        p_buf[s] = exps
        a_buf[s] = scores
        scaled = scores * (1.0 / jnp.sum(scores, axis=0, keepdims=True))
        return rows + fold(scaled), probs + fold(exps)

    rows, probs = lax.fori_loop(0, N_Z, first, (zero, zero))
    got = total(0, jnp.concatenate([rows, probs], axis=0))
    row_scale = 1.0 / got[:CLIPS]
    prob_scale = twice(1.0 / got[CLIPS:])
    for step in (1, 2):
        wide_scale = twice(row_scale)

        def again(s, rows):
            scores = a_buf[s]
            scale = 1.0 / jnp.sum(scores * wide_scale, axis=0, keepdims=True)
            v_buf[s] = jnp.broadcast_to(scale, (8, COLS))
            return rows + fold(scores * scale)

        rows = lax.fori_loop(0, N_Z, again, zero)
        row_scale = 1.0 / total(step, jnp.concatenate([rows, rows], axis=0))[:CLIPS]
    wide_scale = twice(row_scale)

    def assigned(s):
        return a_buf[s] * v_buf[s][0:1] * wide_scale

    def grads(s, carry):
        logit_grad = (PROTOS * (p_buf[s] * prob_scale - assigned(s))).astype(BF16)
        g_buf[s] = logit_grad
        return carry + dot(logit_grad, proto_all[s], NT)

    grad_unit = lax.fori_loop(0, N_Z, grads, jnp.zeros((CLIPS, BOT), F32))
    for p in range(N_CAM):
        gu_send[p] = grad_unit[p * 8 : (p + 1) * 8]
    loop(1, N_R, lambda o: gu_copy(o).start())
    gu_recv[here] = gu_send[cam]

    codes_out[...] = PROTOS * assigned(z)
    grad_proto = dot(unit_b, g_buf[z], TN)
    proto = pr[...].astype(F32)
    col_norm = jnp.sqrt(jnp.sum(proto * proto, axis=0, keepdims=True) + NORM_EPS)
    unit_proto = proto / col_norm
    proto_out[...] = (
        grad_proto - unit_proto * jnp.sum(unit_proto * grad_proto, axis=0, keepdims=True)
    ) / col_norm

    loop(1, N_R, lambda o: gu_copy(o).wait_recv())
    grad8 = jnp.sum(gu_recv[...], axis=0)
    mine = pl.ds(pl.multiple_of(cam * 8, 8), 8)
    unit8 = unit_buf[mine, :]
    grad8 = (grad8 - unit8 * jnp.sum(unit8 * grad8, axis=1, keepdims=True)) / norm_buf[mine, :]
    gz_send[...] = grad8.astype(BF16).astype(F32)
    loop(1, N_CAM, lambda o: gz_copy(o).start())
    gz_recv[cam] = gz_send[...]
    loop(1, N_CLIP, lambda o: side_copy(o).wait_recv())
    pooled_all = jnp.concatenate([side_recv[:, b, :] for b in range(PAIR)], axis=0).astype(BF16)
    loop(1, N_CAM, lambda o: gz_copy(o).wait_recv())
    grad_z = gz_recv[...].reshape(CLIPS, BOT).astype(BF16)

    part = pl.ds(pl.multiple_of(lax.rem(clip * SHARE, LANES), SHARE), SHARE)
    proj_tmp[...] = dot(pooled_all, grad_z, TN)
    proj_out[...] = proj_tmp[part, :]
    grad_pooled = dot(grad_z, wp[pl.ds(pl.multiple_of(cam * LANES, LANES), LANES), :], NT).astype(BF16)
    by_head = []
    for head in range(PAIR):
        mix_all = jnp.concatenate([side_recv[:, 2 + PAIR * b + head, :] for b in range(PAIR)], axis=0)
        high = mix_all.astype(BF16)
        low = (mix_all - high.astype(F32)).astype(BF16)
        by_head.append(dot(high, grad_pooled, TN) + dot(low, grad_pooled, TN))
    lane = lax.broadcasted_iota(jnp.int32, (LANES, LANES), 1)
    value_tmp[...] = jnp.where(lane < HD, by_head[0], by_head[1])
    value_out[...] = value_tmp[part, :]

    for b in range(PAIR):
        loop(1, N_CAM, lambda o: qk_copy(b, o).wait_send())
    loop(1, N_Z, lambda o: proto_copy(o).wait_send())
    for copy in (w_copy, pool_copy, mix_copy, gz_copy):
        loop(1, N_CAM, lambda o: copy(o).wait_send())
    for copy in (z_copy, side_copy):
        loop(1, N_CLIP, lambda o: copy(o).wait_send())
    loop(1, N_R, lambda o: gu_copy(o).wait_send())
    for step in range(3):
        loop(1, N_R, lambda o: row_copy(step, o).wait_send())


def local(tokens, w_query, w_key, w_value, w_proj, prototypes):
    vmem, dma = pltpu.VMEM, pltpu.SemaphoreType.DMA
    codes, proto_grad, proj_grad, value_grad = pl.pallas_call(
        kernel,
        out_shape=(
            jax.ShapeDtypeStruct((CLIPS, COLS), F32),
            jax.ShapeDtypeStruct((BOT, COLS), F32),
            jax.ShapeDtypeStruct((SHARE, BOT), F32),
            jax.ShapeDtypeStruct((SHARE, LANES), F32),
        ),
        in_specs=[pl.BlockSpec(memory_space=pl.ANY)] * 6,
        out_specs=[pl.BlockSpec(memory_space=pltpu.VMEM)] * 4,
        scratch_shapes=[
            vmem((PAIR * TOK, D), BF16), vmem((D, D), BF16), vmem((D, D), BF16), vmem((D, D), BF16),
            vmem((D, BOT), BF16), vmem((BOT, COLS), BF16),
            vmem((N_Z, BOT, COLS), BF16),
            vmem((PAIR, N_CAM, 2, TOK, LANES), BF16), vmem((PAIR, N_CAM, 2, TOK, LANES), BF16),
            vmem((PAIR * PAIR, 8, KEYS), F32),
            vmem((N_CAM, 8, TOK), F32), vmem((N_CAM, 8, TOK), F32),
            vmem((N_CAM, PAIR * PAIR, D), F32), vmem((N_CAM, PAIR * PAIR, D), F32),
            vmem((PAIR * N_CAM, LANES), F32), vmem((N_CAM, PAIR * N_CAM, LANES), F32),
            vmem((4, LANES), F32), vmem((N_CLIP, 4, LANES), F32),
            vmem((N_CAM, 8, LANES), F32), vmem((N_CLIP, 8, LANES), F32),
            vmem((N_Z, CLIPS, COLS), F32), vmem((N_Z, CLIPS, COLS), F32), vmem((N_Z, 8, COLS), F32),
            vmem((N_Z, CLIPS, COLS), BF16), vmem((CLIPS, BOT), F32), vmem((CLIPS, BOT), F32),
            vmem((3, 8, LANES), F32), vmem((3, N_R, 8, LANES), F32),
            vmem((N_CAM, 8, BOT), F32), vmem((N_R, 8, BOT), F32),
            vmem((8, BOT), F32), vmem((N_CAM, 8, BOT), F32),
            vmem((LANES, BOT), F32), vmem((LANES, LANES), F32),
            dma((6,)), dma((PAIR,)), dma((PAIR, N_CAM)), dma((PAIR, N_CAM)), dma((4, N_CAM)), dma((4, N_CAM)),
            dma((N_Z,)), dma((N_Z,)), dma((6, N_CLIP)), dma((6, N_CLIP)),
        ],
        compiler_params=pltpu.CompilerParams(
            collective_id=0, has_side_effects=True, vmem_limit_bytes=58 * 2**20
        ),
    )(tokens.reshape(PAIR * TOK, D), w_query, w_key, w_value, w_proj, prototypes)
    codes = codes.reshape(PAIR, N_CLIP, COLS).transpose(1, 0, 2).reshape(CLIPS, COLS)
    return codes, proto_grad, proj_grad, value_grad


def solution(mesh):
    assert mesh.shape["cam"] == N_CAM and mesh.shape["clip"] == N_CLIP
    in_specs = (P("clip", "cam", None, None), P(), P(), P(), P(), P(None, ("cam", "clip")))
    out_specs = (
        P(None, ("cam", "clip")),
        P(None, ("cam", "clip")),
        P("clip", None),
        P("clip", "cam"),
    )
    return jax.shard_map(local, mesh=mesh, in_specs=in_specs, out_specs=out_specs, check_vma=False)
```

```python
import functools

import jax
import jax.numpy as jnp
from jax import lax
from jax.experimental import pallas as pl
from jax.experimental.pallas import tpu as pltpu
from jax.sharding import PartitionSpec as P

D = 1024
HD = 64
H = 16
BOT = 256
PROTOS = 65536
TOK = 256
CLIPS = 64
N_CAM = 8
N_CLIP = 32
N_Z = 8
N_Y = N_CLIP // N_Z
N_R = N_CAM * N_Y
PAIR = 2
LANES = 128
COLS = PROTOS // (N_CAM * N_CLIP)
SHARE = D // N_CLIP
KEYS = N_CAM * TOK
PIECES = 4
PIECE = TOK // PIECES
ROWS = N_CAM * PIECE

SINK_EPS = 0.05
SOFTMAX_TEMP = 0.1
NORM_EPS = 1e-06
LOG2_E = 1.4426950408889634

MESH = pl.DeviceIdType.MESH
F32 = jnp.float32
BF16 = jnp.bfloat16


CAM_ORDER = (4, 3, 5, 2, 6, 7, 1)
Y_ORDER = (2, 1, 3, 0)
Z_ORDER = (4, 3, 5, 2, 6, 1, 7, 0)
CLIP_ORDER = tuple((oy, oz) for oy in Y_ORDER for oz in Z_ORDER if (oy, oz) != (0, 0))
R_ORDER = tuple((oy, oc) for oy in Y_ORDER for oc in CAM_ORDER + (0,) if (oy, oc) != (0, 0))


def dot(a, b, dims):
    return lax.dot_general(a, b, (dims, ((), ())), preferred_element_type=F32)


NN = ((1,), (0,))
NT = ((1,), (1,))
TN = ((0,), (0,))


def fold(a):
    return a[:, :LANES] + a[:, LANES:]


def twice(a):
    return jnp.concatenate([a, a], axis=1)


def kernel(
    x_in, wq_in, wk_in, wv_in, wp_in, pr_in,
    codes_out, proto_out, proj_out, value_out,
    xv, wq, wk, wv, wp, pr,
    proto_all, k_send, k_recv, q_send, q_recv, acc,
    w_send, w_recv, mix_send, mix_recv, pool_send, pool_recv,
    z_send, z_recv, side_send, side_recv,
    a_buf, p_buf, v_buf, g_buf, unit_buf, norm_buf,
    row_send, row_recv, gu_send, gu_recv, gz_send, gz_recv,
    proj_tmp, value_tmp,
    load_sem, own_sem, y_sem, qk_ss, qk_rs, cam_ss, cam_rs, proto_ss, proto_rs, wide_ss, wide_rs,
):
    cam = lax.axis_index("cam")
    clip = lax.axis_index("clip")
    y, z = lax.div(clip, N_Z), lax.rem(clip, N_Z)
    here = y * N_CAM + cam

    def cam_peer(o):
        return (lax.rem(cam + o, N_CAM), clip)

    def yz_peer(oy, oz):
        return (cam, lax.rem(y + oy, N_Y) * N_Z + lax.rem(z + oz, N_Z))

    def r_peer(oy, oc):
        return (lax.rem(cam + oc, N_CAM), lax.rem(y + oy, N_Y) * N_Z + z)

    def loop(lo, hi, step):
        def body(i, carry):
            step(i)
            return carry

        lax.fori_loop(lo, hi, body, 0)

    barrier = pltpu.get_barrier_semaphore()
    for oz in Z_ORDER[:-1]:
        pl.semaphore_signal(barrier, inc=1, device_id=yz_peer(0, oz), device_id_type=MESH)
    for oy in Y_ORDER[:-1]:
        pl.semaphore_signal(barrier, inc=1, device_id=yz_peer(oy, 0), device_id_type=MESH)
    for o in CAM_ORDER:
        pl.semaphore_signal(barrier, inc=1, device_id=cam_peer(o), device_id_type=MESH)

    loads = [
        pltpu.make_async_copy(x_in.at[pl.ds(0, TOK)], xv.at[pl.ds(0, TOK)], load_sem.at[0]),
        pltpu.make_async_copy(wk_in, wk, load_sem.at[1]),
        pltpu.make_async_copy(wq_in, wq, load_sem.at[2]),
        pltpu.make_async_copy(x_in.at[pl.ds(TOK, TOK)], xv.at[pl.ds(TOK, TOK)], load_sem.at[3]),
        pltpu.make_async_copy(pr_in, pr, load_sem.at[4]),
        pltpu.make_async_copy(wv_in, wv, load_sem.at[5]),
        pltpu.make_async_copy(wp_in, wp, load_sem.at[6]),
    ]
    for load in loads:
        load.start()

    def project_keys(b):
        rows = xv[b * TOK : (b + 1) * TOK, :]
        for j in range(D // 256):
            got = dot(rows, wk[:, j * 256 : (j + 1) * 256], NN).astype(BF16)
            k_send[b, 2 * j] = got[:, :LANES]
            k_send[b, 2 * j + 1] = got[:, LANES:]

    def project_queries(b):
        rows = xv[b * TOK : (b + 1) * TOK, :]
        for j in range(D // 256):
            got = dot(rows, wq[:, j * 256 : (j + 1) * 256], NN).astype(BF16)
            q_send[b, 2 * j] = got[:, :LANES].reshape(PIECES, PIECE, LANES)
            q_send[b, 2 * j + 1] = got[:, LANES:].reshape(PIECES, PIECE, LANES)

    def remote(src, dst, send_sem, recv_sem, to):
        return pltpu.make_async_remote_copy(
            src_ref=src, dst_ref=dst, send_sem=send_sem, recv_sem=recv_sem,
            device_id=to, device_id_type=MESH,
        )

    def k_copy(b, o):
        to = cam_peer(o)
        return remote(k_send.at[b, to[0]], k_recv.at[b, cam], qk_ss.at[b, PIECES, o], qk_rs.at[b, PIECES, o], to)

    def q_copy(b, part, o):
        to = cam_peer(o)
        return remote(
            q_send.at[b, to[0], part], q_recv.at[b, part, cam], qk_ss.at[b, part, o], qk_rs.at[b, part, o], to
        )

    def own_k(b):
        return pltpu.make_async_copy(k_send.at[b, cam], k_recv.at[b, cam], own_sem.at[b, PIECES])

    def own_q(b, part):
        return pltpu.make_async_copy(q_send.at[b, cam, part], q_recv.at[b, part, cam], own_sem.at[b, part])

    def send_keys(b):
        for o in CAM_ORDER:
            k_copy(b, o).start()
        own_k(b).start()

    def send_queries(b):
        for part in range(PIECES):
            for o in CAM_ORDER:
                q_copy(b, part, o).start()
            own_q(b, part).start()

    def proto_copy(i):
        return remote(proto_all.at[z], proto_all.at[z], proto_ss.at[i], proto_rs.at[i], yz_peer(0, Z_ORDER[i]))

    loads[0].wait()
    loads[1].wait()
    project_keys(0)
    pl.semaphore_wait(barrier, N_CAM - 1 + N_Y - 1 + N_Z - 1)
    send_keys(0)
    for oy in Y_ORDER[:-1]:
        pl.semaphore_signal(y_sem, inc=1, device_id=yz_peer(oy, 0), device_id_type=MESH)
    loads[2].wait()
    project_queries(0)
    send_queries(0)
    loads[3].wait()
    project_keys(1)
    send_keys(1)
    project_queries(1)
    send_queries(1)

    loads[4].wait()
    proto = pr[...].astype(F32)
    col_norm = jnp.sqrt(jnp.sum(proto * proto, axis=0, keepdims=True) + NORM_EPS)
    proto_all[z] = (proto / col_norm).astype(BF16)
    for i in range(N_Z - 1):
        proto_copy(i).start()

    acc[...] = jnp.zeros_like(acc)
    lane_q = lax.broadcasted_iota(jnp.int32, (ROWS, LANES), 1)

    def attend(b):
        loop(1, N_CAM, lambda o: k_copy(b, o).wait_recv())
        own_k(b).wait()

        def piece(part):
            loop(1, N_CAM, lambda o: q_copy(b, part, o).wait_recv())
            own_q(b, part).wait()
            keys = k_recv[b].reshape(KEYS, LANES)
            both = q_recv[b, part].reshape(ROWS, LANES)
            for head in range(PAIR):
                rows = jnp.where((lane_q < HD) == (head == 0), both, jnp.zeros_like(both))
                weights = jnp.exp2(dot(rows, keys, NT) * (HD ** (-0.5) * LOG2_E))
                weights = weights * (1.0 / jnp.sum(weights, axis=1, keepdims=True))
                acc[b * PAIR + head] += jnp.sum(weights.reshape(ROWS // 8, 8, KEYS), axis=0)

        loop(0, PIECES, piece)

    loop(0, PAIR, attend)

    class Exchange:
        def __init__(self, order, peer, src, dst, send_sem, recv_sem):
            self.order, self.peer, self.src, self.dst = order, peer, src, dst
            self.send_sem, self.recv_sem = send_sem, recv_sem

        def copy(self, i, to):
            return remote(self.src(to), self.dst, self.send_sem(i), self.recv_sem(i), to)

        def start(self):
            for i, o in enumerate(self.order):
                self.copy(i, self.peer(o)).start()

        def landed(self):
            to = self.peer(self.order[0])
            loop(0, len(self.order), lambda i: self.copy(i, to).wait_recv())

        def left(self):
            to = self.peer(self.order[0])
            loop(0, len(self.order), lambda i: self.copy(i, to).wait_send())

    def cam_exchange(k, src, dst):
        return Exchange(CAM_ORDER, cam_peer, src, dst, lambda i: cam_ss.at[k, i], lambda i: cam_rs.at[k, i])

    def wide_exchange(k, order, peer, src, dst):
        return Exchange(
            order, lambda o: peer(*o), src, dst, lambda i: wide_ss.at[k, i], lambda i: wide_rs.at[k, i]
        )

    w_out = cam_exchange(0, lambda to: w_send.at[to[0]], w_recv.at[cam])
    pool_out = cam_exchange(1, lambda to: pool_send, pool_recv.at[cam])
    mix_out = cam_exchange(2, lambda to: mix_send.at[to[0]], mix_recv.at[cam])
    gz_out = cam_exchange(3, lambda to: gz_send, gz_recv.at[cam])
    z_out = wide_exchange(0, CLIP_ORDER, yz_peer, lambda to: z_send, z_recv.at[clip])
    side_out = wide_exchange(
        1, CLIP_ORDER, yz_peer, lambda to: side_send.at[lax.div(to[1] * SHARE, LANES)], side_recv.at[clip]
    )
    gu_out = wide_exchange(2, R_ORDER, r_peer, lambda to: gu_send.at[to[0]], gu_recv.at[here])

    def row_exchange(step):
        return wide_exchange(3 + step, R_ORDER, r_peer, lambda to: row_send.at[step], row_recv.at[step, here])

    row_out = [row_exchange(step) for step in range(3)]

    row8 = lax.broadcasted_iota(jnp.int32, (8, KEYS), 0)
    weights = jnp.zeros((8, KEYS), F32)
    for r in range(PAIR * PAIR):
        weights = jnp.where(row8 == r, jnp.sum(acc[r], axis=0, keepdims=True) * (1.0 / KEYS), weights)
    for p in range(N_CAM):
        w_send[p] = weights[:, p * TOK : (p + 1) * TOK]
    w_out.start()
    w_recv[cam] = w_send[cam]
    loads[5].wait()
    w_out.landed()

    key_weight = w_recv[...].reshape(8 * N_CAM, TOK).astype(BF16)
    mix0 = dot(key_weight, xv[:TOK, :], NN)
    mix1 = dot(key_weight, xv[TOK:, :], NN)
    row64 = lax.broadcasted_iota(jnp.int32, (8 * N_CAM, D), 0)
    mixture = jnp.where(lax.rem(row64, 8) >= PAIR, mix1, mix0).astype(BF16)
    head_out = dot(mixture, wv[...], NN)
    lane8 = lax.broadcasted_iota(jnp.int32, (8, LANES), 1)
    sub8 = lax.broadcasted_iota(jnp.int32, (8, LANES), 0)
    own_head = lax.rem(sub8, PAIR) == lax.div(lane8, HD)
    for p in range(N_CAM):
        tile = head_out[p * 8 : (p + 1) * 8, p * LANES : (p + 1) * LANES]
        tile = jnp.where(own_head, tile, 0.0)
        pool_send[p : p + 1, :] = tile[0:1] + tile[1:2]
        pool_send[N_CAM + p : N_CAM + p + 1, :] = tile[2:3] + tile[3:4]
    pool_out.start()
    pool_recv[cam] = pool_send[...]
    mixture_f = mixture.astype(F32)
    for p in range(N_CAM):
        mix_send[p] = mixture_f[p * 8 : p * 8 + PAIR * PAIR, :]
    mix_out.start()
    mix_recv[cam] = mix_send[cam]
    loads[6].wait()
    pool_out.landed()
    pooled = jnp.sum(pool_recv[...], axis=0).astype(BF16)
    row16 = lax.broadcasted_iota(jnp.int32, (PAIR * N_CAM, LANES), 0)
    spread = jnp.concatenate(
        [jnp.where(lax.rem(row16, N_CAM) == p, pooled, jnp.zeros_like(pooled)) for p in range(N_CAM)], axis=1
    )
    z_rows = dot(spread, wp[...], NN)
    for b in range(PAIR):
        z_clip = jnp.sum(z_rows[b * N_CAM : (b + 1) * N_CAM], axis=0, keepdims=True)
        for j in range(2):
            z_send[2 * b + j : 2 * b + j + 1, :] = z_clip[:, j * LANES : (j + 1) * LANES]
    pl.semaphore_wait(y_sem, N_Y - 1)
    z_out.start()
    z_recv[clip] = z_send[...]

    mix_out.landed()
    mix_sum = jnp.sum(mix_recv[...], axis=0)
    pooled_f = pooled.astype(F32)
    for p in range(N_CAM):
        side_send[p, 0:1, :] = pooled_f[p : p + 1]
        side_send[p, 1:2, :] = pooled_f[N_CAM + p : N_CAM + p + 1]
        side_send[p, 2:6, :] = mix_sum[:, p * LANES : (p + 1) * LANES]
        side_send[p, 6:8, :] = jnp.zeros((2, LANES), F32)
    for i in range(N_Z - 1):
        proto_copy(i).wait_recv()
    z_out.landed()
    side_out.start()
    side_recv[clip] = side_send[lax.div(clip * SHARE, LANES)]

    embed = jnp.concatenate(
        [jnp.concatenate([z_recv[:, 2 * b + j, :] for j in range(2)], axis=1) for b in range(PAIR)], axis=0
    )
    norm = jnp.sqrt(jnp.sum(embed * embed, axis=1, keepdims=True) + NORM_EPS)
    unit = embed / norm
    unit_buf[...] = unit
    norm_buf[...] = jnp.broadcast_to(norm, norm_buf.shape)
    unit_b = unit.astype(BF16)

    def total(step, sums):
        tall = jnp.broadcast_to(jnp.sum(sums, axis=1, keepdims=True), (LANES, LANES))
        row_send[step] = tall.T[:1, :]
        row_out[step].start()
        row_recv[step, here] = row_send[step]
        row_out[step].landed()
        wide = jnp.sum(row_recv[step], axis=0)
        return jnp.broadcast_to(wide, (LANES, LANES)).T

    zero = jnp.zeros((CLIPS, LANES), F32)

    def first(s, carry):
        rows, probs = carry
        exps = jnp.exp(dot(unit_b, proto_all[s], NN) * (1.0 / SOFTMAX_TEMP))
        scores = exps * exps
        p_buf[s] = exps
        a_buf[s] = scores
        scaled = scores * (1.0 / jnp.sum(scores, axis=0, keepdims=True))
        return rows + fold(scaled), probs + fold(exps)

    rows, probs = lax.fori_loop(0, N_Z, first, (zero, zero))
    got = total(0, jnp.concatenate([rows, probs], axis=0))
    row_scale = 1.0 / got[:CLIPS]
    prob_scale = twice(1.0 / got[CLIPS:])
    for step in (1, 2):
        wide_scale = twice(row_scale)

        def again(s, rows):
            scores = a_buf[s]
            scale = 1.0 / jnp.sum(scores * wide_scale, axis=0, keepdims=True)
            v_buf[s] = jnp.broadcast_to(scale, (8, COLS))
            return rows + fold(scores * scale)

        rows = lax.fori_loop(0, N_Z, again, zero)
        row_scale = 1.0 / total(step, jnp.concatenate([rows, rows], axis=0))[:CLIPS]
    wide_scale = twice(row_scale)

    def assigned(s):
        return a_buf[s] * v_buf[s][0:1] * wide_scale

    def grads(s, carry):
        logit_grad = (PROTOS * (p_buf[s] * prob_scale - assigned(s))).astype(BF16)
        g_buf[s] = logit_grad
        return carry + dot(logit_grad, proto_all[s], NT)

    grad_unit = lax.fori_loop(0, N_Z, grads, jnp.zeros((CLIPS, BOT), F32))
    for p in range(N_CAM):
        gu_send[p] = grad_unit[p * 8 : (p + 1) * 8]
    gu_out.start()
    gu_recv[here] = gu_send[cam]

    codes_out[...] = PROTOS * assigned(z)
    grad_proto = dot(unit_b, g_buf[z], TN)
    proto = pr[...].astype(F32)
    col_norm = jnp.sqrt(jnp.sum(proto * proto, axis=0, keepdims=True) + NORM_EPS)
    unit_proto = proto / col_norm
    proto_out[...] = (
        grad_proto - unit_proto * jnp.sum(unit_proto * grad_proto, axis=0, keepdims=True)
    ) / col_norm

    gu_out.landed()
    grad8 = jnp.sum(gu_recv[...], axis=0)
    mine = pl.ds(pl.multiple_of(cam * 8, 8), 8)
    unit8 = unit_buf[mine, :]
    grad8 = (grad8 - unit8 * jnp.sum(unit8 * grad8, axis=1, keepdims=True)) / norm_buf[mine, :]
    gz_send[...] = grad8.astype(BF16).astype(F32)
    gz_out.start()
    gz_recv[cam] = gz_send[...]
    side_out.landed()
    pooled_all = jnp.concatenate([side_recv[:, b, :] for b in range(PAIR)], axis=0).astype(BF16)
    gz_out.landed()
    grad_z = gz_recv[...].reshape(CLIPS, BOT).astype(BF16)

    part = pl.ds(pl.multiple_of(lax.rem(clip * SHARE, LANES), SHARE), SHARE)
    proj_tmp[...] = dot(pooled_all, grad_z, TN)
    proj_out[...] = proj_tmp[part, :]
    grad_pooled = dot(grad_z, wp[pl.ds(pl.multiple_of(cam * LANES, LANES), LANES), :], NT).astype(BF16)
    by_head = []
    for head in range(PAIR):
        mix_all = jnp.concatenate([side_recv[:, 2 + PAIR * b + head, :] for b in range(PAIR)], axis=0)
        high = mix_all.astype(BF16)
        low = (mix_all - high.astype(F32)).astype(BF16)
        by_head.append(dot(high, grad_pooled, TN) + dot(low, grad_pooled, TN))
    lane = lax.broadcasted_iota(jnp.int32, (LANES, LANES), 1)
    value_tmp[...] = jnp.where(lane < HD, by_head[0], by_head[1])
    value_out[...] = value_tmp[part, :]

    def left(b):
        loop(1, N_CAM, lambda o: k_copy(b, o).wait_send())
        loop(0, PIECES, lambda part: loop(1, N_CAM, lambda o: q_copy(b, part, o).wait_send()))

    loop(0, PAIR, left)
    for i in range(N_Z - 1):
        proto_copy(i).wait_send()
    for out in [w_out, pool_out, mix_out, gz_out, z_out, side_out, gu_out] + row_out:
        out.left()


def finish(codes, proto_grad, proj_grad, value_grad, codes_out, proto_out, proj_out, value_out, order):
    for j in range(COLS // LANES):
        columns = slice(j * LANES, (j + 1) * LANES)
        for b in range(PAIR):
            order[j, pl.ds(b, N_CLIP, stride=PAIR), :] = codes[b * N_CLIP : (b + 1) * N_CLIP, columns]
        codes_out[:, columns] = order[j]
    proto_out[...] = proto_grad[...]
    proj_out[...] = proj_grad[...]
    value_out[...] = value_grad[...]


def local(tokens, w_query, w_key, w_value, w_proj, prototypes):
    vmem, dma = pltpu.VMEM, pltpu.SemaphoreType.DMA
    shapes = (
        jax.ShapeDtypeStruct((CLIPS, COLS), F32),
        jax.ShapeDtypeStruct((BOT, COLS), F32),
        jax.ShapeDtypeStruct((SHARE, BOT), F32),
        jax.ShapeDtypeStruct((SHARE, LANES), F32),
    )
    got = pl.pallas_call(
        kernel,
        out_shape=shapes,
        in_specs=[pl.BlockSpec(memory_space=pl.ANY)] * 6,
        out_specs=[pl.BlockSpec(memory_space=pltpu.VMEM)] * 4,
        scratch_shapes=[
            vmem((PAIR * TOK, D), BF16), vmem((D, D), BF16), vmem((D, D), BF16), vmem((D, D), BF16),
            vmem((D, BOT), BF16), vmem((BOT, COLS), BF16),
            vmem((N_Z, BOT, COLS), BF16),
            vmem((PAIR, N_CAM, TOK, LANES), BF16), vmem((PAIR, N_CAM, TOK, LANES), BF16),
            vmem((PAIR, N_CAM, PIECES, PIECE, LANES), BF16), vmem((PAIR, PIECES, N_CAM, PIECE, LANES), BF16),
            vmem((PAIR * PAIR, 8, KEYS), F32),
            vmem((N_CAM, 8, TOK), F32), vmem((N_CAM, 8, TOK), F32),
            vmem((N_CAM, PAIR * PAIR, D), F32), vmem((N_CAM, PAIR * PAIR, D), F32),
            vmem((PAIR * N_CAM, LANES), F32), vmem((N_CAM, PAIR * N_CAM, LANES), F32),
            vmem((4, LANES), F32), vmem((N_CLIP, 4, LANES), F32),
            vmem((N_CAM, 8, LANES), F32), vmem((N_CLIP, 8, LANES), F32),
            vmem((N_Z, CLIPS, COLS), F32), vmem((N_Z, CLIPS, COLS), F32), vmem((N_Z, 8, COLS), F32),
            vmem((N_Z, CLIPS, COLS), BF16), vmem((CLIPS, BOT), F32), vmem((CLIPS, BOT), F32),
            vmem((3, 1, LANES), F32), vmem((3, N_R, 1, LANES), F32),
            vmem((N_CAM, 8, BOT), F32), vmem((N_R, 8, BOT), F32),
            vmem((8, BOT), F32), vmem((N_CAM, 8, BOT), F32),
            vmem((LANES, BOT), F32), vmem((LANES, LANES), F32),
            dma((7,)), dma((PAIR, PIECES + 1)), pltpu.SemaphoreType.REGULAR,
            dma((PAIR, PIECES + 1, N_CAM)), dma((PAIR, PIECES + 1, N_CAM)), dma((4, N_CAM)), dma((4, N_CAM)),
            dma((N_Z,)), dma((N_Z,)), dma((6, N_CLIP)), dma((6, N_CLIP)),
        ],
        compiler_params=pltpu.CompilerParams(
            collective_id=0, has_side_effects=True, vmem_limit_bytes=58 * 2**20
        ),
    )(tokens.reshape(PAIR * TOK, D), w_query, w_key, w_value, w_proj, prototypes)
    return pl.pallas_call(
        finish,
        out_shape=shapes,
        in_specs=[pl.BlockSpec(memory_space=pltpu.VMEM)] * 4,
        out_specs=[pl.BlockSpec(memory_space=pltpu.VMEM)] * 4,
        scratch_shapes=[vmem((COLS // LANES, CLIPS, LANES), F32)],
    )(*got)


def solution(mesh):
    assert mesh.shape["cam"] == N_CAM and mesh.shape["clip"] == N_CLIP
    in_specs = (P("clip", "cam", None, None), P(), P(), P(), P(), P(None, ("cam", "clip")))
    out_specs = (
        P(None, ("cam", "clip")),
        P(None, ("cam", "clip")),
        P("clip", None),
        P("clip", "cam"),
    )
    return jax.shard_map(local, mesh=mesh, in_specs=in_specs, out_specs=out_specs, check_vma=False)
```

```python
import functools

import jax
import jax.numpy as jnp
from jax import lax
from jax.experimental import pallas as pl
from jax.experimental.pallas import tpu as pltpu
from jax.sharding import PartitionSpec as P

D = 1024
HD = 64
H = 16
BOT = 256
PROTOS = 65536
TOK = 256
CLIPS = 64
N_CAM = 8
N_CLIP = 32
N_Z = 8
N_Y = N_CLIP // N_Z
N_R = N_CAM * N_Y
PAIR = 2
LANES = 128
COLS = PROTOS // (N_CAM * N_CLIP)
SHARE = D // N_CLIP
KEYS = N_CAM * TOK
PIECES = 4
PIECE = TOK // PIECES
ROWS = N_CAM * PIECE

SINK_EPS = 0.05
SOFTMAX_TEMP = 0.1
NORM_EPS = 1e-06
LOG2_E = 1.4426950408889634

MESH = pl.DeviceIdType.MESH
F32 = jnp.float32
BF16 = jnp.bfloat16


CAM_ORDER = (4, 3, 5, 2, 6, 7, 1)
Y_ORDER = (2, 1, 3, 0)
Z_ORDER = (4, 3, 5, 2, 6, 1, 7, 0)
CLIP_ORDER = tuple((oy, oz) for oy in Y_ORDER for oz in Z_ORDER if (oy, oz) != (0, 0))
R_ORDER = tuple((oy, oc) for oy in Y_ORDER for oc in CAM_ORDER + (0,) if (oy, oc) != (0, 0))


def dot(a, b, dims):
    return lax.dot_general(a, b, (dims, ((), ())), preferred_element_type=F32)


NN = ((1,), (0,))
NT = ((1,), (1,))
TN = ((0,), (0,))


def split_dot(a, b):
    high = a.astype(BF16)
    low = (a - high.astype(F32)).astype(BF16)
    got = dot(jnp.concatenate([high, low], axis=0), b, NT)
    return got[: a.shape[0]] + got[a.shape[0] :]


def fold(a):
    return a[:, :LANES] + a[:, LANES:]


def twice(a):
    return jnp.concatenate([a, a], axis=1)


def kernel(
    x_in, wq_in, wk_in, wv_in, wp_in, pr_in,
    codes_out, proto_out, proj_out, value_out,
    xv, wq, wk, wv, wp, pr,
    proto_all, k_send, k_recv, q_send, q_recv, acc,
    w_send, w_recv, mix_send, mix_recv, pool_send, pool_recv,
    z_send, z_recv, side_send, side_recv,
    a_buf, p_buf, unit_buf, norm_buf, prob_buf, scale_buf,
    row_send, row_recv, gs_send, gs_recv, gu_send, gu_recv, gz_send, gz_recv,
    proj_tmp, value_tmp,
    load_sem, own_sem, y_sem, qk_ss, qk_rs, cam_ss, cam_rs, proto_ss, proto_rs, wide_ss, wide_rs,
):
    cam = lax.axis_index("cam")
    clip = lax.axis_index("clip")
    y, z = lax.div(clip, N_Z), lax.rem(clip, N_Z)
    here = y * N_CAM + cam

    def cam_peer(o):
        return (lax.rem(cam + o, N_CAM), clip)

    def yz_peer(oy, oz):
        return (cam, lax.rem(y + oy, N_Y) * N_Z + lax.rem(z + oz, N_Z))

    def r_peer(oy, oc):
        return (lax.rem(cam + oc, N_CAM), lax.rem(y + oy, N_Y) * N_Z + z)

    def loop(lo, hi, step):
        def body(i, carry):
            step(i)
            return carry

        lax.fori_loop(lo, hi, body, 0)

    barrier = pltpu.get_barrier_semaphore()
    for oz in Z_ORDER[:-1]:
        pl.semaphore_signal(barrier, inc=1, device_id=yz_peer(0, oz), device_id_type=MESH)
    for oy in Y_ORDER[:-1]:
        pl.semaphore_signal(barrier, inc=1, device_id=yz_peer(oy, 0), device_id_type=MESH)
    for o in CAM_ORDER:
        pl.semaphore_signal(barrier, inc=1, device_id=cam_peer(o), device_id_type=MESH)

    loads = [
        pltpu.make_async_copy(x_in.at[pl.ds(0, TOK)], xv.at[pl.ds(0, TOK)], load_sem.at[0]),
        pltpu.make_async_copy(wk_in, wk, load_sem.at[1]),
        pltpu.make_async_copy(wq_in, wq, load_sem.at[2]),
        pltpu.make_async_copy(x_in.at[pl.ds(TOK, TOK)], xv.at[pl.ds(TOK, TOK)], load_sem.at[3]),
        pltpu.make_async_copy(pr_in, pr, load_sem.at[4]),
        pltpu.make_async_copy(wv_in, wv, load_sem.at[5]),
        pltpu.make_async_copy(wp_in, wp, load_sem.at[6]),
    ]
    for load in loads:
        load.start()

    def project_keys(b):
        rows = xv[b * TOK : (b + 1) * TOK, :]
        for j in range(D // 256):
            got = dot(rows, wk[:, j * 256 : (j + 1) * 256], NN).astype(BF16)
            k_send[b, 2 * j] = got[:, :LANES]
            k_send[b, 2 * j + 1] = got[:, LANES:]

    def project_queries(b):
        rows = xv[b * TOK : (b + 1) * TOK, :]
        for j in range(D // 256):
            got = dot(rows, wq[:, j * 256 : (j + 1) * 256], NN).astype(BF16)
            q_send[b, 2 * j] = got[:, :LANES].reshape(PIECES, PIECE, LANES)
            q_send[b, 2 * j + 1] = got[:, LANES:].reshape(PIECES, PIECE, LANES)

    def remote(src, dst, send_sem, recv_sem, to):
        return pltpu.make_async_remote_copy(
            src_ref=src, dst_ref=dst, send_sem=send_sem, recv_sem=recv_sem,
            device_id=to, device_id_type=MESH,
        )

    def k_copy(b, o):
        to = cam_peer(o)
        return remote(k_send.at[b, to[0]], k_recv.at[b, cam], qk_ss.at[b, PIECES, o], qk_rs.at[b, PIECES, o], to)

    def q_copy(b, part, o):
        to = cam_peer(o)
        return remote(
            q_send.at[b, to[0], part], q_recv.at[b, part, cam], qk_ss.at[b, part, o], qk_rs.at[b, part, o], to
        )

    def own_k(b):
        return pltpu.make_async_copy(k_send.at[b, cam], k_recv.at[b, cam], own_sem.at[b, PIECES])

    def own_q(b, part):
        return pltpu.make_async_copy(q_send.at[b, cam, part], q_recv.at[b, part, cam], own_sem.at[b, part])

    def send_keys(b):
        for o in CAM_ORDER:
            k_copy(b, o).start()
        own_k(b).start()

    def send_queries(b):
        for part in range(PIECES):
            for o in CAM_ORDER:
                q_copy(b, part, o).start()
            own_q(b, part).start()

    def proto_copy(i):
        return remote(proto_all.at[z], proto_all.at[z], proto_ss.at[i], proto_rs.at[i], yz_peer(0, Z_ORDER[i]))

    loads[0].wait()
    loads[1].wait()
    project_keys(0)
    pl.semaphore_wait(barrier, N_CAM - 1 + N_Y - 1 + N_Z - 1)
    send_keys(0)
    for oy in Y_ORDER[:-1]:
        pl.semaphore_signal(y_sem, inc=1, device_id=yz_peer(oy, 0), device_id_type=MESH)
    loads[2].wait()
    project_queries(0)
    send_queries(0)
    loads[3].wait()
    project_keys(1)
    send_keys(1)
    project_queries(1)
    send_queries(1)

    loads[4].wait()
    proto = pr[...].astype(F32)
    col_norm = jnp.sqrt(jnp.sum(proto * proto, axis=0, keepdims=True) + NORM_EPS)
    proto_all[z] = (proto / col_norm).astype(BF16)
    for i in range(N_Z - 1):
        proto_copy(i).start()

    acc[...] = jnp.zeros_like(acc)
    lane_q = lax.broadcasted_iota(jnp.int32, (ROWS, LANES), 1)

    def attend(b):
        loop(1, N_CAM, lambda o: k_copy(b, o).wait_recv())
        own_k(b).wait()

        def piece(part):
            loop(1, N_CAM, lambda o: q_copy(b, part, o).wait_recv())
            own_q(b, part).wait()
            keys = k_recv[b].reshape(KEYS, LANES)
            both = q_recv[b, part].reshape(ROWS, LANES)
            for head in range(PAIR):
                rows = jnp.where((lane_q < HD) == (head == 0), both, jnp.zeros_like(both))
                weights = jnp.exp2(dot(rows, keys, NT) * (HD ** (-0.5) * LOG2_E))
                weights = weights * (1.0 / jnp.sum(weights, axis=1, keepdims=True))
                acc[b * PAIR + head] += jnp.sum(weights.reshape(ROWS // 8, 8, KEYS), axis=0)

        loop(0, PIECES, piece)

    loop(0, PAIR, attend)

    class Exchange:
        def __init__(self, order, peer, src, slots, mine, send_sem, recv_sem):
            self.order, self.peer, self.src, self.dst = order, peer, src, slots.at[mine]
            self.send_sem, self.recv_sem = send_sem, recv_sem
            others = slots.at[pl.ds(0, len(order))]
            self.whole = remote(others, others, send_sem, recv_sem, peer(order[0]))

        def start(self):
            for o in self.order:
                to = self.peer(o)
                remote(self.src(to), self.dst, self.send_sem, self.recv_sem, to).start()

        def landed(self):
            self.whole.wait_recv()

        def left(self):
            self.whole.wait_send()

    def cam_exchange(k, src, slots):
        return Exchange(CAM_ORDER, cam_peer, src, slots, cam, cam_ss.at[k], cam_rs.at[k])

    def clip_exchange(k, src, slots):
        return Exchange(CLIP_ORDER, lambda o: yz_peer(*o), src, slots, clip, wide_ss.at[k], wide_rs.at[k])

    def r_exchange(k, src, slots):
        return Exchange(R_ORDER, lambda o: r_peer(*o), src, slots, here, wide_ss.at[k], wide_rs.at[k])

    w_out = cam_exchange(0, lambda to: w_send.at[to[0]], w_recv)
    pool_out = cam_exchange(1, lambda to: pool_send, pool_recv)
    mix_out = cam_exchange(2, lambda to: mix_send.at[to[0]], mix_recv)
    gz_out = cam_exchange(3, lambda to: gz_send, gz_recv)
    z_out = clip_exchange(0, lambda to: z_send, z_recv)
    side_out = clip_exchange(1, lambda to: side_send.at[lax.div(to[1] * SHARE, LANES)], side_recv)
    gu_out = r_exchange(2, lambda to: gu_send.at[to[0]], gu_recv)
    gs_out = r_exchange(6, lambda to: gs_send.at[to[0]], gs_recv)

    def row_exchange(step):
        return r_exchange(3 + step, lambda to: row_send.at[step], row_recv.at[step])

    row_out = [row_exchange(step) for step in range(3)]

    row8 = lax.broadcasted_iota(jnp.int32, (8, KEYS), 0)
    weights = jnp.zeros((8, KEYS), F32)
    for r in range(PAIR * PAIR):
        weights = jnp.where(row8 == r, jnp.sum(acc[r], axis=0, keepdims=True) * (1.0 / KEYS), weights)
    for p in range(N_CAM):
        w_send[p] = weights[:, p * TOK : (p + 1) * TOK]
    w_out.start()
    w_recv[cam] = w_send[cam]
    loads[5].wait()
    w_out.landed()

    key_weight = w_recv[...].reshape(8 * N_CAM, TOK).astype(BF16)
    mix0 = dot(key_weight, xv[:TOK, :], NN)
    mix1 = dot(key_weight, xv[TOK:, :], NN)
    row64 = lax.broadcasted_iota(jnp.int32, (8 * N_CAM, D), 0)
    mixture = jnp.where(lax.rem(row64, 8) >= PAIR, mix1, mix0).astype(BF16)
    head_out = dot(mixture, wv[...], NN)
    lane8 = lax.broadcasted_iota(jnp.int32, (8, LANES), 1)
    sub8 = lax.broadcasted_iota(jnp.int32, (8, LANES), 0)
    own_head = lax.rem(sub8, PAIR) == lax.div(lane8, HD)
    for p in range(N_CAM):
        tile = head_out[p * 8 : (p + 1) * 8, p * LANES : (p + 1) * LANES]
        tile = jnp.where(own_head, tile, 0.0)
        pool_send[p : p + 1, :] = tile[0:1] + tile[1:2]
        pool_send[N_CAM + p : N_CAM + p + 1, :] = tile[2:3] + tile[3:4]
    pool_out.start()
    pool_recv[cam] = pool_send[...]
    mixture_f = mixture.astype(F32)
    for p in range(N_CAM):
        mix_send[p] = mixture_f[p * 8 : p * 8 + PAIR * PAIR, :]
    mix_out.start()
    mix_recv[cam] = mix_send[cam]
    loads[6].wait()
    pool_out.landed()
    pooled = jnp.sum(pool_recv[...], axis=0).astype(BF16)
    row16 = lax.broadcasted_iota(jnp.int32, (PAIR * N_CAM, LANES), 0)
    spread = jnp.concatenate(
        [jnp.where(lax.rem(row16, N_CAM) == p, pooled, jnp.zeros_like(pooled)) for p in range(N_CAM)], axis=1
    )
    z_rows = dot(spread, wp[...], NN)
    for b in range(PAIR):
        z_clip = jnp.sum(z_rows[b * N_CAM : (b + 1) * N_CAM], axis=0, keepdims=True)
        for j in range(2):
            z_send[2 * b + j : 2 * b + j + 1, :] = z_clip[:, j * LANES : (j + 1) * LANES]
    pl.semaphore_wait(y_sem, N_Y - 1)
    z_out.start()
    z_recv[clip] = z_send[...]

    def left(b):
        loop(1, N_CAM, lambda o: k_copy(b, o).wait_send())
        loop(0, PIECES, lambda part: loop(1, N_CAM, lambda o: q_copy(b, part, o).wait_send()))

    loop(0, PAIR, left)
    for i in range(N_Z - 1):
        proto_copy(i).wait_send()
    w_out.left()
    pool_out.left()

    mix_out.landed()
    mix_sum = jnp.sum(mix_recv[...], axis=0)
    pooled_f = pooled.astype(F32)
    for p in range(N_CAM):
        side_send[p, 0:1, :] = pooled_f[p : p + 1]
        side_send[p, 1:2, :] = pooled_f[N_CAM + p : N_CAM + p + 1]
        side_send[p, 2:6, :] = mix_sum[:, p * LANES : (p + 1) * LANES]
        side_send[p, 6:8, :] = jnp.zeros((2, LANES), F32)
    for i in range(N_Z - 1):
        proto_copy(i).wait_recv()
    z_out.landed()

    embed = jnp.concatenate(
        [jnp.concatenate([z_recv[:, 2 * b + j, :] for j in range(2)], axis=1) for b in range(PAIR)], axis=0
    )
    norm = jnp.sqrt(jnp.sum(embed * embed, axis=1, keepdims=True) + NORM_EPS)
    unit = embed / norm
    unit_buf[...] = unit
    norm_buf[...] = jnp.broadcast_to(norm, norm_buf.shape)
    unit_b = unit.astype(BF16)

    def total(step, sums, meanwhile=None):
        tall = jnp.broadcast_to(jnp.sum(sums, axis=1, keepdims=True), (LANES, LANES))
        row_send[step] = tall.T[:1, :]
        row_out[step].start()
        row_recv[step, here] = row_send[step]
        if meanwhile is not None:
            meanwhile()
        row_out[step].landed()
        wide = jnp.sum(row_recv[step], axis=0)
        return jnp.broadcast_to(wide, (LANES, LANES)).T

    zero = jnp.zeros((CLIPS, LANES), F32)

    def first(s, carry):
        rows, probs = carry
        exps = jnp.exp(dot(unit_b, proto_all[s], NN) * (1.0 / SOFTMAX_TEMP))
        scores = exps * exps
        p_buf[s] = exps
        a_buf[s] = scores
        scaled = scores * (1.0 / jnp.sum(scores, axis=0, keepdims=True))
        return rows + fold(scaled), probs + fold(exps)

    rows, probs = lax.fori_loop(0, N_Z, first, (zero, zero))

    def spread_rows(send, out, recv, value):
        for p in range(N_CAM):
            send[p] = value[p * 8 : (p + 1) * 8]
        out.start()
        recv[here] = send[cam]

    empty = jnp.zeros((CLIPS, BOT), F32)

    def while_waiting():
        side_out.start()
        side_recv[clip] = side_send[lax.div(clip * SHARE, LANES)]
        soft = lax.fori_loop(0, N_Z, lambda s, sums: sums + split_dot(p_buf[s], proto_all[s]), empty)
        spread_rows(gs_send, gs_out, gs_recv, soft)

    got = total(0, jnp.concatenate([rows, probs], axis=0), while_waiting)
    row_scale = 1.0 / got[:CLIPS]
    prob_scale = 1.0 / got[CLIPS:]
    prob_buf[...] = prob_scale

    def rescale(s, wide_scale):
        scores = a_buf[s]
        return scores * (1.0 / jnp.sum(scores * wide_scale, axis=0, keepdims=True))

    wide_scale = twice(row_scale)
    rows = lax.fori_loop(0, N_Z, lambda s, sums: sums + fold(rescale(s, wide_scale)), zero)
    row_scale = 1.0 / total(1, jnp.concatenate([rows, rows], axis=0))[:CLIPS]
    last_scale = twice(row_scale)

    def last(s, carry):
        rows, sums = carry
        scaled = rescale(s, last_scale)
        a_buf[s] = scaled
        return rows + fold(scaled), sums + split_dot(scaled, proto_all[s])

    rows, hard = lax.fori_loop(0, N_Z, last, (zero, empty))
    spread_rows(gu_send, gu_out, gu_recv, hard)
    row_scale = 1.0 / total(2, jnp.concatenate([rows, rows], axis=0))[:CLIPS]
    scale_buf[...] = row_scale

    mine = pl.ds(pl.multiple_of(cam * 8, 8), 8)
    gs_out.landed()
    grad8 = jnp.sum(gs_recv[...], axis=0) * twice(prob_buf[mine, :])
    gu_out.landed()
    grad8 = PROTOS * (grad8 - jnp.sum(gu_recv[...], axis=0) * twice(scale_buf[mine, :]))
    unit8 = unit_buf[mine, :]
    grad8 = (grad8 - unit8 * jnp.sum(unit8 * grad8, axis=1, keepdims=True)) / norm_buf[mine, :]
    gz_send[...] = grad8.astype(BF16).astype(F32)
    gz_out.start()
    gz_recv[cam] = gz_send[...]

    assigned = a_buf[z] * twice(row_scale)
    codes_out[...] = PROTOS * assigned
    logit_grad = (PROTOS * (p_buf[z] * twice(prob_scale) - assigned)).astype(BF16)
    grad_proto = dot(unit_b, logit_grad, TN)
    proto = pr[...].astype(F32)
    col_norm = jnp.sqrt(jnp.sum(proto * proto, axis=0, keepdims=True) + NORM_EPS)
    unit_proto = proto / col_norm
    proto_out[...] = (
        grad_proto - unit_proto * jnp.sum(unit_proto * grad_proto, axis=0, keepdims=True)
    ) / col_norm

    side_out.landed()
    pooled_all = jnp.concatenate([side_recv[:, b, :] for b in range(PAIR)], axis=0).astype(BF16)
    gz_out.landed()
    grad_z = gz_recv[...].reshape(CLIPS, BOT).astype(BF16)

    part = pl.ds(pl.multiple_of(lax.rem(clip * SHARE, LANES), SHARE), SHARE)
    proj_tmp[...] = dot(pooled_all, grad_z, TN)
    proj_out[...] = proj_tmp[part, :]
    grad_pooled = dot(grad_z, wp[pl.ds(pl.multiple_of(cam * LANES, LANES), LANES), :], NT).astype(BF16)
    by_head = []
    for head in range(PAIR):
        mix_all = jnp.concatenate([side_recv[:, 2 + PAIR * b + head, :] for b in range(PAIR)], axis=0)
        high = mix_all.astype(BF16)
        low = (mix_all - high.astype(F32)).astype(BF16)
        by_head.append(dot(high, grad_pooled, TN) + dot(low, grad_pooled, TN))
    lane = lax.broadcasted_iota(jnp.int32, (LANES, LANES), 1)
    value_tmp[...] = jnp.where(lane < HD, by_head[0], by_head[1])
    value_out[...] = value_tmp[part, :]

    for out in [mix_out, gz_out, z_out, side_out, gs_out, gu_out] + row_out:
        out.left()


def finish(codes, proto_grad, proj_grad, value_grad, codes_out, proto_out, proj_out, value_out, order):
    for j in range(COLS // LANES):
        columns = slice(j * LANES, (j + 1) * LANES)
        for b in range(PAIR):
            order[j, pl.ds(b, N_CLIP, stride=PAIR), :] = codes[b * N_CLIP : (b + 1) * N_CLIP, columns]
        codes_out[:, columns] = order[j]
    proto_out[...] = proto_grad[...]
    proj_out[...] = proj_grad[...]
    value_out[...] = value_grad[...]


def local(tokens, w_query, w_key, w_value, w_proj, prototypes):
    vmem, dma = pltpu.VMEM, pltpu.SemaphoreType.DMA
    shapes = (
        jax.ShapeDtypeStruct((CLIPS, COLS), F32),
        jax.ShapeDtypeStruct((BOT, COLS), F32),
        jax.ShapeDtypeStruct((SHARE, BOT), F32),
        jax.ShapeDtypeStruct((SHARE, LANES), F32),
    )
    got = pl.pallas_call(
        kernel,
        out_shape=shapes,
        in_specs=[pl.BlockSpec(memory_space=pl.ANY)] * 6,
        out_specs=[pl.BlockSpec(memory_space=pltpu.VMEM)] * 4,
        scratch_shapes=[
            vmem((PAIR * TOK, D), BF16), vmem((D, D), BF16), vmem((D, D), BF16), vmem((D, D), BF16),
            vmem((D, BOT), BF16), vmem((BOT, COLS), BF16),
            vmem((N_Z, BOT, COLS), BF16),
            vmem((PAIR, N_CAM, TOK, LANES), BF16), vmem((PAIR, N_CAM, TOK, LANES), BF16),
            vmem((PAIR, N_CAM, PIECES, PIECE, LANES), BF16), vmem((PAIR, PIECES, N_CAM, PIECE, LANES), BF16),
            vmem((PAIR * PAIR, 8, KEYS), F32),
            vmem((N_CAM, 8, TOK), F32), vmem((N_CAM, 8, TOK), F32),
            vmem((N_CAM, PAIR * PAIR, D), F32), vmem((N_CAM, PAIR * PAIR, D), F32),
            vmem((PAIR * N_CAM, LANES), F32), vmem((N_CAM, PAIR * N_CAM, LANES), F32),
            vmem((4, LANES), F32), vmem((N_CLIP, 4, LANES), F32),
            vmem((N_CAM, 8, LANES), F32), vmem((N_CLIP, 8, LANES), F32),
            vmem((N_Z, CLIPS, COLS), F32), vmem((N_Z, CLIPS, COLS), F32),
            vmem((CLIPS, BOT), F32), vmem((CLIPS, BOT), F32), vmem((CLIPS, LANES), F32), vmem((CLIPS, LANES), F32),
            vmem((3, 1, LANES), F32), vmem((3, N_R, 1, LANES), F32),
            vmem((N_CAM, 8, BOT), F32), vmem((N_R, 8, BOT), F32),
            vmem((N_CAM, 8, BOT), F32), vmem((N_R, 8, BOT), F32),
            vmem((8, BOT), F32), vmem((N_CAM, 8, BOT), F32),
            vmem((LANES, BOT), F32), vmem((LANES, LANES), F32),
            dma((7,)), dma((PAIR, PIECES + 1)), pltpu.SemaphoreType.REGULAR,
            dma((PAIR, PIECES + 1, N_CAM)), dma((PAIR, PIECES + 1, N_CAM)), dma((4,)), dma((4,)),
            dma((N_Z,)), dma((N_Z,)), dma((7,)), dma((7,)),
        ],
        compiler_params=pltpu.CompilerParams(
            collective_id=0, has_side_effects=True, vmem_limit_bytes=58 * 2**20
        ),
    )(tokens.reshape(PAIR * TOK, D), w_query, w_key, w_value, w_proj, prototypes)
    return pl.pallas_call(
        finish,
        out_shape=shapes,
        in_specs=[pl.BlockSpec(memory_space=pltpu.VMEM)] * 4,
        out_specs=[pl.BlockSpec(memory_space=pltpu.VMEM)] * 4,
        scratch_shapes=[vmem((COLS // LANES, CLIPS, LANES), F32)],
    )(*got)


def solution(mesh):
    assert mesh.shape["cam"] == N_CAM and mesh.shape["clip"] == N_CLIP
    in_specs = (P("clip", "cam", None, None), P(), P(), P(), P(), P(None, ("cam", "clip")))
    out_specs = (
        P(None, ("cam", "clip")),
        P(None, ("cam", "clip")),
        P("clip", None),
        P("clip", "cam"),
    )
    return jax.shard_map(local, mesh=mesh, in_specs=in_specs, out_specs=out_specs, check_vma=False)
```

```python
import functools

import jax
import jax.numpy as jnp
from jax import lax
from jax.experimental import pallas as pl
from jax.experimental.pallas import tpu as pltpu
from jax.sharding import PartitionSpec as P

D = 1024
HD = 64
H = 16
BOT = 256
PROTOS = 65536
TOK = 256
CLIPS = 64
N_CAM = 8
N_CLIP = 32
N_Z = 8
N_Y = N_CLIP // N_Z
N_R = N_CAM * N_Y
PAIR = 2
LANES = 128
COLS = PROTOS // (N_CAM * N_CLIP)
SHARE = D // N_CLIP
KEYS = N_CAM * TOK
PIECES = 4
PIECE = TOK // PIECES
ROWS = N_CAM * PIECE

VMEM_LIMIT = 58 * 2**20

SINK_EPS = 0.05
SOFTMAX_TEMP = 0.1
NORM_EPS = 1e-06
LOG2_E = 1.4426950408889634

MESH = pl.DeviceIdType.MESH
F32 = jnp.float32
BF16 = jnp.bfloat16


CAM_ORDER = (4, 3, 5, 2, 6, 7, 1)
Y_ORDER = (2, 1, 3, 0)
Z_ORDER = (4, 3, 5, 2, 6, 1, 7, 0)
CLIP_ORDER = tuple((oy, oz) for oy in Y_ORDER for oz in Z_ORDER if (oy, oz) != (0, 0))
R_ORDER = tuple((oy, oc) for oy in Y_ORDER for oc in CAM_ORDER + (0,) if (oy, oc) != (0, 0))


def dot(a, b, dims):
    return lax.dot_general(a, b, (dims, ((), ())), preferred_element_type=F32)


NN = ((1,), (0,))
NT = ((1,), (1,))
TN = ((0,), (0,))


def split_dot(a, b):
    high = a.astype(BF16)
    low = (a - high.astype(F32)).astype(BF16)
    got = dot(jnp.concatenate([high, low], axis=0), b, NT)
    return got[: a.shape[0]] + got[a.shape[0] :]


def fold(a):
    return a[:, :LANES] + a[:, LANES:]


def twice(a):
    return jnp.concatenate([a, a], axis=1)


def kernel(
    x_in, wq_in, wk_in, wv_in, wp_in, pr_in,
    codes_out, proto_out, proj_out, value_out,
    xv, wq, wk, wv, wp, pr,
    proto_all, k_send, k_recv, q_send, q_recv, acc,
    w_send, w_recv, mix_send, mix_recv, pool_send, pool_recv,
    z_send, z_recv, side_send, side_recv,
    a_buf, p_buf, unit_buf, norm_buf, prob_buf, scale_buf,
    row_send, row_recv, gs_send, gs_recv, gu_send, gu_recv, gz_send, gz_recv,
    side_tmp,
    load_sem, own_sem, y_sem, qk_ss, qk_rs, cam_ss, cam_rs, proto_ss, proto_rs, wide_ss, wide_rs,
):
    cam = lax.axis_index("cam")
    clip = lax.axis_index("clip")
    y, z = lax.div(clip, N_Z), lax.rem(clip, N_Z)
    here = y * N_CAM + cam

    cams = [cam] + [lax.rem(cam + o, N_CAM) for o in range(1, N_CAM)]
    lines = [lax.rem(y + o, N_Y) * N_Z for o in range(N_Y)]
    depths = [z] + [lax.rem(z + o, N_Z) for o in range(1, N_Z)]

    def cam_peer(o):
        return (cams[o], clip)

    def yz_peer(oy, oz):
        return (cam, lines[oy] + depths[oz])

    def r_peer(oy, oc):
        return (cams[oc], lines[oy] + z)

    def loop(lo, hi, step):
        def body(i, carry):
            step(i)
            return carry

        lax.fori_loop(lo, hi, body, 0)

    barrier = pltpu.get_barrier_semaphore()
    for oz in Z_ORDER[:-1]:
        pl.semaphore_signal(barrier, inc=1, device_id=yz_peer(0, oz), device_id_type=MESH)
    for oy in Y_ORDER[:-1]:
        pl.semaphore_signal(barrier, inc=1, device_id=yz_peer(oy, 0), device_id_type=MESH)
    for o in CAM_ORDER:
        pl.semaphore_signal(barrier, inc=1, device_id=cam_peer(o), device_id_type=MESH)

    loads = [
        pltpu.make_async_copy(x_in.at[pl.ds(0, TOK)], xv.at[pl.ds(0, TOK)], load_sem.at[0]),
        pltpu.make_async_copy(wk_in, wk, load_sem.at[1]),
        pltpu.make_async_copy(wq_in, wq, load_sem.at[2]),
        pltpu.make_async_copy(x_in.at[pl.ds(TOK, TOK)], xv.at[pl.ds(TOK, TOK)], load_sem.at[3]),
        pltpu.make_async_copy(pr_in, pr, load_sem.at[4]),
        pltpu.make_async_copy(wv_in, wv, load_sem.at[5]),
        pltpu.make_async_copy(wp_in, wp, load_sem.at[6]),
    ]
    for load in loads[:2]:
        load.start()

    def project_keys(b):
        rows = xv[b * TOK : (b + 1) * TOK, :]
        for j in range(D // 256):
            got = dot(rows, wk[:, j * 256 : (j + 1) * 256], NN).astype(BF16)
            k_send[b, 2 * j] = got[:, :LANES]
            k_send[b, 2 * j + 1] = got[:, LANES:]

    def project_queries(b):
        rows = xv[b * TOK : (b + 1) * TOK, :]
        for j in range(D // 256):
            got = dot(rows, wq[:, j * 256 : (j + 1) * 256], NN).astype(BF16)
            q_send[b, 2 * j] = got[:, :LANES].reshape(PIECES, PIECE, LANES)
            q_send[b, 2 * j + 1] = got[:, LANES:].reshape(PIECES, PIECE, LANES)

    def remote(src, dst, send_sem, recv_sem, to):
        return pltpu.make_async_remote_copy(
            src_ref=src, dst_ref=dst, send_sem=send_sem, recv_sem=recv_sem,
            device_id=to, device_id_type=MESH,
        )

    def k_copy(b, o):
        to = cam_peer(o)
        return remote(k_send.at[b, to[0]], k_recv.at[b, cam], qk_ss.at[b, PIECES, o], qk_rs.at[b, PIECES, o], to)

    def q_copy(b, part, o):
        to = cam_peer(o)
        return remote(
            q_send.at[b, to[0], part], q_recv.at[b, part, cam], qk_ss.at[b, part, o], qk_rs.at[b, part, o], to
        )

    def own_k(b):
        return pltpu.make_async_copy(k_send.at[b, cam], k_recv.at[b, cam], own_sem.at[b, PIECES])

    def own_q(b, part):
        return pltpu.make_async_copy(q_send.at[b, cam, part], q_recv.at[b, part, cam], own_sem.at[b, part])

    def send_keys(b):
        for o in CAM_ORDER:
            k_copy(b, o).start()
        own_k(b).start()

    def send_queries(b):
        for part in range(PIECES):
            for o in CAM_ORDER:
                q_copy(b, part, o).start()
            own_q(b, part).start()

    def proto_copy(i):
        return remote(proto_all.at[z], proto_all.at[z], proto_ss.at[i], proto_rs.at[i], yz_peer(0, Z_ORDER[i]))

    loads[0].wait()
    loads[1].wait()
    for load in loads[2:]:
        load.start()
    project_keys(0)
    pl.semaphore_wait(barrier, N_CAM - 1 + N_Y - 1 + N_Z - 1)
    send_keys(0)
    for oy in Y_ORDER[:-1]:
        pl.semaphore_signal(y_sem, inc=1, device_id=yz_peer(oy, 0), device_id_type=MESH)
    loads[2].wait()
    project_queries(0)
    send_queries(0)
    loads[3].wait()
    project_keys(1)
    send_keys(1)
    project_queries(1)
    send_queries(1)

    loads[4].wait()
    proto = pr[...].astype(F32)
    col_norm = jnp.sqrt(jnp.sum(proto * proto, axis=0, keepdims=True) + NORM_EPS)
    proto_all[z] = (proto / col_norm).astype(BF16)
    for i in range(N_Z - 1):
        proto_copy(i).start()

    acc[...] = jnp.zeros_like(acc)
    lane_q = lax.broadcasted_iota(jnp.int32, (ROWS, LANES), 1)

    def attend(b):
        for o in CAM_ORDER[::-1]:
            k_copy(b, o).wait_recv()
        own_k(b).wait()

        def piece(part):
            for o in CAM_ORDER[::-1]:
                q_copy(b, part, o).wait_recv()
            own_q(b, part).wait()
            keys = k_recv[b].reshape(KEYS, LANES)
            both = q_recv[b, part].reshape(ROWS, LANES)
            for head in range(PAIR):
                rows = jnp.where((lane_q < HD) == (head == 0), both, jnp.zeros_like(both))
                weights = jnp.exp2(dot(rows, keys, NT) * (HD ** (-0.5) * LOG2_E))
                weights = weights * (1.0 / jnp.sum(weights, axis=1, keepdims=True))
                acc[b * PAIR + head] += jnp.sum(weights.reshape(ROWS // 8, 8, KEYS), axis=0)

        loop(0, PIECES, piece)

    loop(0, PAIR, attend)

    class Exchange:
        def __init__(self, order, peer, src, slots, mine, send_sem, recv_sem):
            self.order, self.peer, self.src, self.dst = order, peer, src, slots.at[mine]
            self.send_sem, self.recv_sem = send_sem, recv_sem
            others = slots.at[pl.ds(0, len(order))]
            self.whole = remote(others, others, send_sem, recv_sem, peer(order[0]))

        def start(self):
            for o in self.order:
                to = self.peer(o)
                remote(self.src(to), self.dst, self.send_sem, self.recv_sem, to).start()

        def landed(self):
            self.whole.wait_recv()

        def left(self):
            self.whole.wait_send()

    def cam_exchange(k, src, slots):
        return Exchange(CAM_ORDER, cam_peer, src, slots, cam, cam_ss.at[k], cam_rs.at[k])

    def clip_exchange(k, src, slots):
        return Exchange(CLIP_ORDER, lambda o: yz_peer(*o), src, slots, clip, wide_ss.at[k], wide_rs.at[k])

    def r_exchange(k, src, slots):
        return Exchange(R_ORDER, lambda o: r_peer(*o), src, slots, here, wide_ss.at[k], wide_rs.at[k])

    w_out = cam_exchange(0, lambda to: w_send.at[to[0]], w_recv)
    pool_out = cam_exchange(1, lambda to: pool_send, pool_recv)
    mix_out = cam_exchange(2, lambda to: mix_send.at[to[0]], mix_recv)
    gz_out = cam_exchange(3, lambda to: gz_send, gz_recv)
    z_out = clip_exchange(0, lambda to: z_send, z_recv)
    side_out = clip_exchange(1, lambda to: side_send.at[lax.div(to[1] * SHARE, LANES)], side_recv)
    gu_out = r_exchange(2, lambda to: gu_send.at[to[0]], gu_recv)
    gs_out = r_exchange(6, lambda to: gs_send.at[to[0]], gs_recv)

    def row_exchange(step):
        return r_exchange(3 + step, lambda to: row_send.at[step], row_recv.at[step])

    row_out = [row_exchange(step) for step in range(3)]

    row8 = lax.broadcasted_iota(jnp.int32, (8, KEYS), 0)
    weights = jnp.zeros((8, KEYS), F32)
    for r in range(PAIR * PAIR):
        weights = jnp.where(row8 == r, jnp.sum(acc[r], axis=0, keepdims=True) * (1.0 / KEYS), weights)
    for p in range(N_CAM):
        w_send[p] = weights[:, p * TOK : (p + 1) * TOK]
    w_out.start()
    w_recv[cam] = w_send[cam]
    loads[5].wait()
    w_out.landed()

    key_weight = w_recv[...].reshape(8 * N_CAM, TOK).astype(BF16)
    mix0 = dot(key_weight, xv[:TOK, :], NN)
    mix1 = dot(key_weight, xv[TOK:, :], NN)
    row64 = lax.broadcasted_iota(jnp.int32, (8 * N_CAM, D), 0)
    mixture = jnp.where(lax.rem(row64, 8) >= PAIR, mix1, mix0).astype(BF16)
    head_out = dot(mixture, wv[...], NN)
    lane8 = lax.broadcasted_iota(jnp.int32, (8, LANES), 1)
    sub8 = lax.broadcasted_iota(jnp.int32, (8, LANES), 0)
    own_head = lax.rem(sub8, PAIR) == lax.div(lane8, HD)
    for p in range(N_CAM):
        tile = head_out[p * 8 : (p + 1) * 8, p * LANES : (p + 1) * LANES]
        tile = jnp.where(own_head, tile, 0.0)
        pool_send[p : p + 1, :] = tile[0:1] + tile[1:2]
        pool_send[N_CAM + p : N_CAM + p + 1, :] = tile[2:3] + tile[3:4]
    pool_out.start()
    pool_recv[cam] = pool_send[...]
    mixture_f = mixture.astype(F32)
    for p in range(N_CAM):
        mix_send[p] = mixture_f[p * 8 : p * 8 + PAIR * PAIR, :]
    mix_out.start()
    mix_recv[cam] = mix_send[cam]
    loads[6].wait()
    pool_out.landed()
    pooled = jnp.sum(pool_recv[...], axis=0).astype(BF16)
    row16 = lax.broadcasted_iota(jnp.int32, (PAIR * N_CAM, LANES), 0)
    spread = jnp.concatenate(
        [jnp.where(lax.rem(row16, N_CAM) == p, pooled, jnp.zeros_like(pooled)) for p in range(N_CAM)], axis=1
    )
    z_rows = dot(spread, wp[...], NN)
    for b in range(PAIR):
        z_clip = jnp.sum(z_rows[b * N_CAM : (b + 1) * N_CAM], axis=0, keepdims=True)
        for j in range(2):
            z_send[2 * b + j : 2 * b + j + 1, :] = z_clip[:, j * LANES : (j + 1) * LANES]
    pl.semaphore_wait(y_sem, N_Y - 1)
    z_out.start()
    z_recv[clip] = z_send[...]

    def left(b):
        for o in CAM_ORDER:
            k_copy(b, o).wait_send()

        def part_left(part):
            for o in CAM_ORDER:
                q_copy(b, part, o).wait_send()

        loop(0, PIECES, part_left)

    loop(0, PAIR, left)
    for i in range(N_Z - 1):
        proto_copy(i).wait_send()
    w_out.left()
    pool_out.left()

    mix_out.landed()
    mix_sum = jnp.sum(mix_recv[...], axis=0)
    pooled_f = pooled.astype(F32)
    for p in range(N_CAM):
        side_send[p, 0:1, :] = pooled_f[p : p + 1]
        side_send[p, 1:2, :] = pooled_f[N_CAM + p : N_CAM + p + 1]
        side_send[p, 2:6, :] = mix_sum[:, p * LANES : (p + 1) * LANES]
        side_send[p, 6:8, :] = jnp.zeros((2, LANES), F32)
    for i in range(N_Z - 1):
        proto_copy(i).wait_recv()
    z_out.landed()

    embed = jnp.concatenate(
        [jnp.concatenate([z_recv[:, 2 * b + j, :] for j in range(2)], axis=1) for b in range(PAIR)], axis=0
    )
    norm = jnp.sqrt(jnp.sum(embed * embed, axis=1, keepdims=True) + NORM_EPS)
    unit = embed / norm
    unit_buf[...] = unit
    norm_buf[...] = jnp.broadcast_to(norm, norm_buf.shape)
    unit_b = unit.astype(BF16)

    def total(step, sums, meanwhile=None):
        tall = jnp.broadcast_to(jnp.sum(sums, axis=1, keepdims=True), (LANES, LANES))
        row_send[step] = tall.T[:1, :]
        row_out[step].start()
        row_recv[step, here] = row_send[step]
        if meanwhile is not None:
            meanwhile()
        row_out[step].landed()
        wide = jnp.sum(row_recv[step], axis=0)
        return jnp.broadcast_to(wide, (LANES, LANES)).T

    zero = jnp.zeros((CLIPS, LANES), F32)

    def first(s, carry):
        rows, probs = carry
        exps = jnp.exp(dot(unit_b, proto_all[s], NN) * (1.0 / SOFTMAX_TEMP))
        scores = exps * exps
        p_buf[s] = exps
        a_buf[s] = scores
        scaled = scores * (1.0 / jnp.sum(scores, axis=0, keepdims=True))
        return rows + fold(scaled), probs + fold(exps)

    rows, probs = lax.fori_loop(0, N_Z, first, (zero, zero), unroll=True)

    def spread_rows(send, out, recv, value):
        for p in range(N_CAM):
            send[p] = value[p * 8 : (p + 1) * 8]
        out.start()
        recv[here] = send[cam]

    empty = jnp.zeros((CLIPS, BOT), F32)

    def while_waiting():
        side_out.start()
        side_recv[clip] = side_send[lax.div(clip * SHARE, LANES)]
        soft = lax.fori_loop(0, N_Z, lambda s, sums: sums + split_dot(p_buf[s], proto_all[s]), empty, unroll=True)
        spread_rows(gs_send, gs_out, gs_recv, soft)

    got = total(0, jnp.concatenate([rows, probs], axis=0), while_waiting)
    row_scale = 1.0 / got[:CLIPS]
    prob_scale = 1.0 / got[CLIPS:]
    prob_buf[...] = prob_scale

    def rescale(s, wide_scale):
        scores = a_buf[s]
        return scores * (1.0 / jnp.sum(scores * wide_scale, axis=0, keepdims=True))

    wide_scale = twice(row_scale)
    rows = lax.fori_loop(0, N_Z, lambda s, sums: sums + fold(rescale(s, wide_scale)), zero, unroll=True)
    row_scale = 1.0 / total(1, jnp.concatenate([rows, rows], axis=0))[:CLIPS]
    last_scale = twice(row_scale)

    def last(s, carry):
        rows, sums = carry
        scaled = rescale(s, last_scale)
        a_buf[s] = scaled
        return rows + fold(scaled), sums + split_dot(scaled, proto_all[s])

    rows, hard = lax.fori_loop(0, N_Z, last, (zero, empty), unroll=True)
    spread_rows(gu_send, gu_out, gu_recv, hard)
    row_scale = 1.0 / total(2, jnp.concatenate([rows, rows], axis=0))[:CLIPS]
    scale_buf[...] = row_scale

    mine = pl.ds(pl.multiple_of(cam * 8, 8), 8)
    gs_out.landed()
    grad8 = jnp.sum(gs_recv[...], axis=0) * twice(prob_buf[mine, :])
    gu_out.landed()
    grad8 = PROTOS * (grad8 - jnp.sum(gu_recv[...], axis=0) * twice(scale_buf[mine, :]))
    unit8 = unit_buf[mine, :]
    grad8 = (grad8 - unit8 * jnp.sum(unit8 * grad8, axis=1, keepdims=True)) / norm_buf[mine, :]
    gz_send[...] = grad8.astype(BF16).astype(F32)
    gz_out.start()
    gz_recv[cam] = gz_send[...]

    assigned = a_buf[z] * twice(row_scale)
    codes_out[...] = PROTOS * assigned
    logit_grad = (PROTOS * (p_buf[z] * twice(prob_scale) - assigned)).astype(BF16)
    grad_proto = dot(unit_b, logit_grad, TN)
    proto = pr[...].astype(F32)
    col_norm = jnp.sqrt(jnp.sum(proto * proto, axis=0, keepdims=True) + NORM_EPS)
    unit_proto = proto / col_norm
    proto_out[...] = (
        grad_proto - unit_proto * jnp.sum(unit_proto * grad_proto, axis=0, keepdims=True)
    ) / col_norm

    side_out.landed()
    part = pl.ds(pl.multiple_of(lax.rem(clip * SHARE, LANES), SHARE), SHARE)

    def features(row):
        tall = jnp.concatenate([side_recv[:, row(b), :] for b in range(PAIR)], axis=0).T
        side_tmp[:, :CLIPS] = tall
        return side_tmp[part, :][:, :CLIPS]

    pooled_all = features(lambda b: b).astype(BF16)
    parts = []
    for head in range(PAIR):
        mix_all = features(lambda b: 2 + PAIR * b + head)
        high = mix_all.astype(BF16)
        parts += [high, (mix_all - high.astype(F32)).astype(BF16)]
    mix_parts = jnp.concatenate(parts, axis=0)

    gz_out.landed()
    grad_z = gz_recv[...].reshape(CLIPS, BOT).astype(BF16)
    proj_out[...] = dot(pooled_all, grad_z, NN)
    grad_pooled = dot(grad_z, wp[pl.ds(pl.multiple_of(cam * LANES, LANES), LANES), :], NT).astype(BF16)
    by_head = dot(mix_parts, grad_pooled, NN)
    lane = lax.broadcasted_iota(jnp.int32, (SHARE, LANES), 1)
    value_out[...] = jnp.where(
        lane < HD,
        by_head[:SHARE] + by_head[SHARE : 2 * SHARE],
        by_head[2 * SHARE : 3 * SHARE] + by_head[3 * SHARE :],
    )

    for out in [mix_out, gz_out, z_out, side_out, gs_out, gu_out] + row_out:
        out.left()


def finish(codes, proto_grad, proj_grad, value_grad, codes_out, proto_out, proj_out, value_out, order):
    for j in range(COLS // LANES):
        columns = slice(j * LANES, (j + 1) * LANES)
        for b in range(PAIR):
            order[j, pl.ds(b, N_CLIP, stride=PAIR), :] = codes[b * N_CLIP : (b + 1) * N_CLIP, columns]
        codes_out[:, columns] = order[j]
    proto_out[...] = proto_grad[...]
    proj_out[...] = proj_grad[...]
    value_out[...] = value_grad[...]


def local(tokens, w_query, w_key, w_value, w_proj, prototypes):
    vmem, dma = pltpu.VMEM, pltpu.SemaphoreType.DMA
    shapes = (
        jax.ShapeDtypeStruct((CLIPS, COLS), F32),
        jax.ShapeDtypeStruct((BOT, COLS), F32),
        jax.ShapeDtypeStruct((SHARE, BOT), F32),
        jax.ShapeDtypeStruct((SHARE, LANES), F32),
    )
    got = pl.pallas_call(
        kernel,
        out_shape=shapes,
        in_specs=[pl.BlockSpec(memory_space=pl.ANY)] * 6,
        out_specs=[pl.BlockSpec(memory_space=pltpu.VMEM)] * 4,
        scratch_shapes=[
            vmem((PAIR * TOK, D), BF16), vmem((D, D), BF16), vmem((D, D), BF16), vmem((D, D), BF16),
            vmem((D, BOT), BF16), vmem((BOT, COLS), BF16),
            vmem((N_Z, BOT, COLS), BF16),
            vmem((PAIR, N_CAM, TOK, LANES), BF16), vmem((PAIR, N_CAM, TOK, LANES), BF16),
            vmem((PAIR, N_CAM, PIECES, PIECE, LANES), BF16), vmem((PAIR, PIECES, N_CAM, PIECE, LANES), BF16),
            vmem((PAIR * PAIR, 8, KEYS), F32),
            vmem((N_CAM, 8, TOK), F32), vmem((N_CAM, 8, TOK), F32),
            vmem((N_CAM, PAIR * PAIR, D), F32), vmem((N_CAM, PAIR * PAIR, D), F32),
            vmem((PAIR * N_CAM, LANES), F32), vmem((N_CAM, PAIR * N_CAM, LANES), F32),
            vmem((4, LANES), F32), vmem((N_CLIP, 4, LANES), F32),
            vmem((N_CAM, 8, LANES), F32), vmem((N_CLIP, 8, LANES), F32),
            vmem((N_Z, CLIPS, COLS), F32), vmem((N_Z, CLIPS, COLS), F32),
            vmem((CLIPS, BOT), F32), vmem((CLIPS, BOT), F32), vmem((CLIPS, LANES), F32), vmem((CLIPS, LANES), F32),
            vmem((3, 1, LANES), F32), vmem((3, N_R, 1, LANES), F32),
            vmem((N_CAM, 8, BOT), F32), vmem((N_R, 8, BOT), F32),
            vmem((N_CAM, 8, BOT), F32), vmem((N_R, 8, BOT), F32),
            vmem((8, BOT), F32), vmem((N_CAM, 8, BOT), F32),
            vmem((LANES, LANES), F32),
            dma((7,)), dma((PAIR, PIECES + 1)), pltpu.SemaphoreType.REGULAR,
            dma((PAIR, PIECES + 1, N_CAM)), dma((PAIR, PIECES + 1, N_CAM)), dma((4,)), dma((4,)),
            dma((N_Z,)), dma((N_Z,)), dma((7,)), dma((7,)),
        ],
        compiler_params=pltpu.CompilerParams(
            collective_id=0, has_side_effects=True, vmem_limit_bytes=VMEM_LIMIT
        ),
    )(tokens.reshape(PAIR * TOK, D), w_query, w_key, w_value, w_proj, prototypes)
    return pl.pallas_call(
        finish,
        out_shape=shapes,
        in_specs=[pl.BlockSpec(memory_space=pltpu.VMEM)] * 4,
        out_specs=[pl.BlockSpec(memory_space=pltpu.VMEM)] * 4,
        scratch_shapes=[vmem((COLS // LANES, CLIPS, LANES), F32)],
    )(*got)


def solution(mesh):
    assert mesh.shape["cam"] == N_CAM and mesh.shape["clip"] == N_CLIP
    in_specs = (P("clip", "cam", None, None), P(), P(), P(), P(), P(None, ("cam", "clip")))
    out_specs = (
        P(None, ("cam", "clip")),
        P(None, ("cam", "clip")),
        P("clip", None),
        P("clip", "cam"),
    )
    return jax.shard_map(local, mesh=mesh, in_specs=in_specs, out_specs=out_specs, check_vma=False)
```

```python
import functools

import jax
import jax.numpy as jnp
from jax import lax
from jax.experimental import pallas as pl
from jax.experimental.pallas import tpu as pltpu
from jax.sharding import PartitionSpec as P

D = 1024
HD = 64
H = 16
BOT = 256
PROTOS = 65536
TOK = 256
CLIPS = 64
N_CAM = 8
N_CLIP = 32
N_Z = 8
N_Y = N_CLIP // N_Z
N_R = N_CAM * N_Y
PAIR = 2
LANES = 128
COLS = PROTOS // (N_CAM * N_CLIP)
SHARE = D // N_CLIP
KEYS = N_CAM * TOK
PIECES = 4
PIECE = TOK // PIECES
ROWS = N_CAM * PIECE

VMEM_LIMIT = 58 * 2**20

SINK_EPS = 0.05
SOFTMAX_TEMP = 0.1
NORM_EPS = 1e-06
LOG2_E = 1.4426950408889634

MESH = pl.DeviceIdType.MESH
F32 = jnp.float32
BF16 = jnp.bfloat16


CAM_ORDER = (4, 3, 5, 2, 6, 7, 1)
Y_ORDER = (2, 1, 3, 0)
Z_ORDER = (4, 3, 5, 2, 6, 1, 7, 0)
CLIP_ORDER = tuple((oy, oz) for oy in Y_ORDER for oz in Z_ORDER if (oy, oz) != (0, 0))
R_ORDER = tuple((oy, oc) for oy in Y_ORDER for oc in CAM_ORDER + (0,) if (oy, oc) != (0, 0))


def dot(a, b, dims):
    return lax.dot_general(a, b, (dims, ((), ())), preferred_element_type=F32)


NN = ((1,), (0,))
NT = ((1,), (1,))
TN = ((0,), (0,))


def split_dot(a, b):
    high = a.astype(BF16)
    low = (a - high.astype(F32)).astype(BF16)
    got = dot(jnp.concatenate([high, low], axis=0), b, NT)
    return got[: a.shape[0]] + got[a.shape[0] :]


def fold(a):
    return a[:, :LANES] + a[:, LANES:]


def twice(a):
    return jnp.concatenate([a, a], axis=1)


def kernel(
    x_in, wq_in, wk_in, wv_in, wp_in, pr_in,
    codes_out, proto_out, proj_out, value_out,
    xv, wq, wk, wv, wp, pr,
    proto_all, k_send, k_recv, q_send, q_recv, acc,
    w_send, w_recv, mix_send, mix_recv, pool_send, pool_recv,
    z_send, z_recv, side_send, side_recv,
    a_buf, p_buf, unit_buf, norm_buf, prob_buf, scale_buf,
    row_send, row_recv, gs_send, gs_recv, gu_send, gu_recv, gz_send, gz_recv,
    side_tmp,
    load_sem, own_sem, y_sem, qk_ss, qk_rs, cam_ss, cam_rs, proto_ss, proto_rs, wide_ss, wide_rs,
):
    cam = lax.axis_index("cam")
    clip = lax.axis_index("clip")
    y, z = lax.div(clip, N_Z), lax.rem(clip, N_Z)
    here = y * N_CAM + cam

    cams = [cam] + [lax.rem(cam + o, N_CAM) for o in range(1, N_CAM)]
    lines = [lax.rem(y + o, N_Y) * N_Z for o in range(N_Y)]
    depths = [z] + [lax.rem(z + o, N_Z) for o in range(1, N_Z)]

    def cam_peer(o):
        return (cams[o], clip)

    def yz_peer(oy, oz):
        return (cam, lines[oy] + depths[oz])

    def r_peer(oy, oc):
        return (cams[oc], lines[oy] + z)

    def loop(lo, hi, step):
        def body(i, carry):
            step(i)
            return carry

        lax.fori_loop(lo, hi, body, 0)

    barrier = pltpu.get_barrier_semaphore()
    for oz in Z_ORDER[:-1]:
        pl.semaphore_signal(barrier, inc=1, device_id=yz_peer(0, oz), device_id_type=MESH)
    for oy in Y_ORDER[:-1]:
        pl.semaphore_signal(barrier, inc=1, device_id=yz_peer(oy, 0), device_id_type=MESH)
    for o in CAM_ORDER:
        pl.semaphore_signal(barrier, inc=1, device_id=cam_peer(o), device_id_type=MESH)

    loads = [
        pltpu.make_async_copy(x_in.at[pl.ds(0, TOK)], xv.at[pl.ds(0, TOK)], load_sem.at[0]),
        pltpu.make_async_copy(wk_in, wk, load_sem.at[1]),
        pltpu.make_async_copy(wq_in, wq, load_sem.at[2]),
        pltpu.make_async_copy(x_in.at[pl.ds(TOK, TOK)], xv.at[pl.ds(TOK, TOK)], load_sem.at[3]),
        pltpu.make_async_copy(pr_in, pr, load_sem.at[4]),
        pltpu.make_async_copy(wv_in, wv, load_sem.at[5]),
        pltpu.make_async_copy(wp_in, wp, load_sem.at[6]),
    ]
    for load in loads[:2]:
        load.start()

    def project_keys(b):
        rows = xv[b * TOK : (b + 1) * TOK, :]
        for j in range(D // 256):
            got = dot(rows, wk[:, j * 256 : (j + 1) * 256], NN).astype(BF16)
            k_send[b, 2 * j] = got[:, :LANES]
            k_send[b, 2 * j + 1] = got[:, LANES:]

    def project_queries(b):
        rows = xv[b * TOK : (b + 1) * TOK, :]
        for j in range(D // 256):
            got = dot(rows, wq[:, j * 256 : (j + 1) * 256], NN).astype(BF16)
            q_send[b, 2 * j] = got[:, :LANES].reshape(PIECES, PIECE, LANES)
            q_send[b, 2 * j + 1] = got[:, LANES:].reshape(PIECES, PIECE, LANES)

    def remote(src, dst, send_sem, recv_sem, to):
        return pltpu.make_async_remote_copy(
            src_ref=src, dst_ref=dst, send_sem=send_sem, recv_sem=recv_sem,
            device_id=to, device_id_type=MESH,
        )

    def k_copy(b, o):
        to = cam_peer(o)
        return remote(k_send.at[b, to[0]], k_recv.at[b, cam], qk_ss.at[b, PIECES, o], qk_rs.at[b, PIECES, o], to)

    def q_copy(b, part, o):
        to = cam_peer(o)
        return remote(
            q_send.at[b, to[0], part], q_recv.at[b, part, cam], qk_ss.at[b, part, o], qk_rs.at[b, part, o], to
        )

    def own_k(b):
        return pltpu.make_async_copy(k_send.at[b, cam], k_recv.at[b, cam], own_sem.at[b, PIECES])

    def own_q(b, part):
        return pltpu.make_async_copy(q_send.at[b, cam, part], q_recv.at[b, part, cam], own_sem.at[b, part])

    def send_keys(b):
        for o in CAM_ORDER:
            k_copy(b, o).start()
        own_k(b).start()

    def send_queries(b, part):
        for o in CAM_ORDER:
            q_copy(b, part, o).start()
        own_q(b, part).start()

    def proto_copy(i):
        return remote(proto_all.at[z], proto_all.at[z], proto_ss.at[i], proto_rs.at[i], yz_peer(0, Z_ORDER[i]))

    loads[0].wait()
    loads[1].wait()
    for load in loads[2:]:
        load.start()
    project_keys(0)
    pl.semaphore_wait(barrier, N_CAM - 1 + N_Y - 1 + N_Z - 1)
    send_keys(0)
    for oy in Y_ORDER[:-1]:
        pl.semaphore_signal(y_sem, inc=1, device_id=yz_peer(oy, 0), device_id_type=MESH)
    loads[2].wait()
    project_queries(0)
    send_queries(0, 0)
    send_queries(0, 1)
    loads[3].wait()
    project_keys(1)
    project_queries(1)

    loads[4].wait()
    proto = pr[...].astype(F32)
    col_norm = jnp.sqrt(jnp.sum(proto * proto, axis=0, keepdims=True) + NORM_EPS)
    proto_all[z] = (proto / col_norm).astype(BF16)
    for i in range(N_Z - 1):
        proto_copy(i).start()

    acc[...] = jnp.zeros_like(acc)
    lane_q = lax.broadcasted_iota(jnp.int32, (ROWS, LANES), 1)

    def attend(b, sends):
        for o in CAM_ORDER[::-1]:
            k_copy(b, o).wait_recv()
        own_k(b).wait()

        def piece(part):
            for o in CAM_ORDER[::-1]:
                q_copy(b, part, o).wait_recv()
            own_q(b, part).wait()
            for at, blocks in sends.items():

                @pl.when(part == at)
                def _():
                    for send in blocks:
                        send()

            keys = k_recv[b].reshape(KEYS, LANES)
            both = q_recv[b, part].reshape(ROWS, LANES)
            for head in range(PAIR):
                rows = jnp.where((lane_q < HD) == (head == 0), both, jnp.zeros_like(both))
                weights = jnp.exp2(dot(rows, keys, NT) * (HD ** (-0.5) * LOG2_E))
                weights = weights * (1.0 / jnp.sum(weights, axis=1, keepdims=True))
                acc[b * PAIR + head] += jnp.sum(weights.reshape(ROWS // 8, 8, KEYS), axis=0)

        loop(0, PIECES, piece)

    def queries(b, part):
        return functools.partial(send_queries, b, part)

    attend(0, {0: (queries(0, 2), queries(0, 3)), 1: (functools.partial(send_keys, 1),), 3: (queries(1, 0),)})
    attend(1, {0: (queries(1, 1), queries(1, 2)), 1: (queries(1, 3),)})

    class Exchange:
        def __init__(self, order, peer, src, slots, mine, send_sem, recv_sem):
            self.order, self.peer, self.src, self.dst = order, peer, src, slots.at[mine]
            self.send_sem, self.recv_sem = send_sem, recv_sem
            others = slots.at[pl.ds(0, len(order))]
            self.whole = remote(others, others, send_sem, recv_sem, peer(order[0]))

        def start(self):
            for o in self.order:
                to = self.peer(o)
                remote(self.src(to), self.dst, self.send_sem, self.recv_sem, to).start()

        def landed(self):
            self.whole.wait_recv()

        def left(self):
            self.whole.wait_send()

    def cam_exchange(k, src, slots):
        return Exchange(CAM_ORDER, cam_peer, src, slots, cam, cam_ss.at[k], cam_rs.at[k])

    def clip_exchange(k, src, slots):
        return Exchange(CLIP_ORDER, lambda o: yz_peer(*o), src, slots, clip, wide_ss.at[k], wide_rs.at[k])

    def r_exchange(k, src, slots):
        return Exchange(R_ORDER, lambda o: r_peer(*o), src, slots, here, wide_ss.at[k], wide_rs.at[k])

    w_out = cam_exchange(0, lambda to: w_send.at[to[0]], w_recv)
    pool_out = cam_exchange(1, lambda to: pool_send, pool_recv)
    mix_out = cam_exchange(2, lambda to: mix_send.at[to[0]], mix_recv)
    gz_out = cam_exchange(3, lambda to: gz_send, gz_recv)
    z_out = clip_exchange(0, lambda to: z_send, z_recv)
    side_out = clip_exchange(1, lambda to: side_send.at[lax.div(to[1] * SHARE, LANES)], side_recv)
    gu_out = r_exchange(2, lambda to: gu_send.at[to[0]], gu_recv)
    gs_out = r_exchange(6, lambda to: gs_send.at[to[0]], gs_recv)

    def row_exchange(step):
        return r_exchange(3 + step, lambda to: row_send.at[step], row_recv.at[step])

    row_out = [row_exchange(step) for step in range(3)]

    row8 = lax.broadcasted_iota(jnp.int32, (8, KEYS), 0)
    weights = jnp.zeros((8, KEYS), F32)
    for r in range(PAIR * PAIR):
        weights = jnp.where(row8 == r, jnp.sum(acc[r], axis=0, keepdims=True) * (1.0 / KEYS), weights)
    for p in range(N_CAM):
        w_send[p] = weights[:, p * TOK : (p + 1) * TOK]
    w_out.start()
    w_recv[cam] = w_send[cam]
    loads[5].wait()
    w_out.landed()

    key_weight = w_recv[...].reshape(8 * N_CAM, TOK).astype(BF16)
    mix0 = dot(key_weight, xv[:TOK, :], NN)
    mix1 = dot(key_weight, xv[TOK:, :], NN)
    row64 = lax.broadcasted_iota(jnp.int32, (8 * N_CAM, D), 0)
    mixture = jnp.where(lax.rem(row64, 8) >= PAIR, mix1, mix0).astype(BF16)
    head_out = dot(mixture, wv[...], NN)
    lane8 = lax.broadcasted_iota(jnp.int32, (8, LANES), 1)
    sub8 = lax.broadcasted_iota(jnp.int32, (8, LANES), 0)
    own_head = lax.rem(sub8, PAIR) == lax.div(lane8, HD)
    for p in range(N_CAM):
        tile = head_out[p * 8 : (p + 1) * 8, p * LANES : (p + 1) * LANES]
        tile = jnp.where(own_head, tile, 0.0)
        pool_send[p : p + 1, :] = tile[0:1] + tile[1:2]
        pool_send[N_CAM + p : N_CAM + p + 1, :] = tile[2:3] + tile[3:4]
    pool_out.start()
    pool_recv[cam] = pool_send[...]
    mixture_f = mixture.astype(F32)
    for p in range(N_CAM):
        mix_send[p] = mixture_f[p * 8 : p * 8 + PAIR * PAIR, :]
    mix_out.start()
    mix_recv[cam] = mix_send[cam]
    loads[6].wait()
    pool_out.landed()
    pooled = jnp.sum(pool_recv[...], axis=0).astype(BF16)
    row16 = lax.broadcasted_iota(jnp.int32, (PAIR * N_CAM, LANES), 0)
    spread = jnp.concatenate(
        [jnp.where(lax.rem(row16, N_CAM) == p, pooled, jnp.zeros_like(pooled)) for p in range(N_CAM)], axis=1
    )
    z_rows = dot(spread, wp[...], NN)
    for b in range(PAIR):
        z_clip = jnp.sum(z_rows[b * N_CAM : (b + 1) * N_CAM], axis=0, keepdims=True)
        for j in range(2):
            z_send[2 * b + j : 2 * b + j + 1, :] = z_clip[:, j * LANES : (j + 1) * LANES]
    pl.semaphore_wait(y_sem, N_Y - 1)
    z_out.start()
    z_recv[clip] = z_send[...]

    def left(b):
        for o in CAM_ORDER:
            k_copy(b, o).wait_send()

        def part_left(part):
            for o in CAM_ORDER:
                q_copy(b, part, o).wait_send()

        loop(0, PIECES, part_left)

    loop(0, PAIR, left)
    for i in range(N_Z - 1):
        proto_copy(i).wait_send()
    w_out.left()
    pool_out.left()

    mix_out.landed()
    mix_sum = jnp.sum(mix_recv[...], axis=0)
    pooled_f = pooled.astype(F32)
    for p in range(N_CAM):
        side_send[p, 0:1, :] = pooled_f[p : p + 1]
        side_send[p, 1:2, :] = pooled_f[N_CAM + p : N_CAM + p + 1]
        side_send[p, 2:6, :] = mix_sum[:, p * LANES : (p + 1) * LANES]
        side_send[p, 6:8, :] = jnp.zeros((2, LANES), F32)
    for i in range(N_Z - 1):
        proto_copy(i).wait_recv()
    z_out.landed()

    embed = jnp.concatenate(
        [jnp.concatenate([z_recv[:, 2 * b + j, :] for j in range(2)], axis=1) for b in range(PAIR)], axis=0
    )
    norm = jnp.sqrt(jnp.sum(embed * embed, axis=1, keepdims=True) + NORM_EPS)
    unit = embed / norm
    unit_buf[...] = unit
    norm_buf[...] = jnp.broadcast_to(norm, norm_buf.shape)
    unit_b = unit.astype(BF16)

    def total(step, sums, meanwhile=None):
        tall = jnp.broadcast_to(jnp.sum(sums, axis=1, keepdims=True), (LANES, LANES))
        row_send[step] = tall.T[:1, :]
        row_out[step].start()
        row_recv[step, here] = row_send[step]
        if meanwhile is not None:
            meanwhile()
        row_out[step].landed()
        wide = jnp.sum(row_recv[step], axis=0)
        return jnp.broadcast_to(wide, (LANES, LANES)).T

    zero = jnp.zeros((CLIPS, LANES), F32)

    def first(s, carry):
        rows, probs = carry
        exps = jnp.exp(dot(unit_b, proto_all[s], NN) * (1.0 / SOFTMAX_TEMP))
        scores = exps * exps
        p_buf[s] = exps
        a_buf[s] = scores
        scaled = scores * (1.0 / jnp.sum(scores, axis=0, keepdims=True))
        return rows + fold(scaled), probs + fold(exps)

    rows, probs = lax.fori_loop(0, N_Z, first, (zero, zero), unroll=True)

    def spread_rows(send, out, recv, value):
        for p in range(N_CAM):
            send[p] = value[p * 8 : (p + 1) * 8]
        out.start()
        recv[here] = send[cam]

    empty = jnp.zeros((CLIPS, BOT), F32)

    def while_waiting():
        side_out.start()
        side_recv[clip] = side_send[lax.div(clip * SHARE, LANES)]
        soft = lax.fori_loop(0, N_Z, lambda s, sums: sums + split_dot(p_buf[s], proto_all[s]), empty, unroll=True)
        spread_rows(gs_send, gs_out, gs_recv, soft)

    got = total(0, jnp.concatenate([rows, probs], axis=0), while_waiting)
    row_scale = 1.0 / got[:CLIPS]
    prob_scale = 1.0 / got[CLIPS:]
    prob_buf[...] = prob_scale

    def rescale(s, wide_scale):
        scores = a_buf[s]
        return scores * (1.0 / jnp.sum(scores * wide_scale, axis=0, keepdims=True))

    wide_scale = twice(row_scale)
    rows = lax.fori_loop(0, N_Z, lambda s, sums: sums + fold(rescale(s, wide_scale)), zero, unroll=True)
    row_scale = 1.0 / total(1, jnp.concatenate([rows, rows], axis=0))[:CLIPS]
    last_scale = twice(row_scale)

    def last(s, carry):
        rows, sums = carry
        scaled = rescale(s, last_scale)
        a_buf[s] = scaled
        return rows + fold(scaled), sums + split_dot(scaled, proto_all[s])

    rows, hard = lax.fori_loop(0, N_Z, last, (zero, empty), unroll=True)
    spread_rows(gu_send, gu_out, gu_recv, hard)
    row_scale = 1.0 / total(2, jnp.concatenate([rows, rows], axis=0))[:CLIPS]
    scale_buf[...] = row_scale

    mine = pl.ds(pl.multiple_of(cam * 8, 8), 8)
    gs_out.landed()
    grad8 = jnp.sum(gs_recv[...], axis=0) * twice(prob_buf[mine, :])
    gu_out.landed()
    grad8 = PROTOS * (grad8 - jnp.sum(gu_recv[...], axis=0) * twice(scale_buf[mine, :]))
    unit8 = unit_buf[mine, :]
    grad8 = (grad8 - unit8 * jnp.sum(unit8 * grad8, axis=1, keepdims=True)) / norm_buf[mine, :]
    gz_send[...] = grad8.astype(BF16).astype(F32)
    gz_out.start()
    gz_recv[cam] = gz_send[...]

    assigned = a_buf[z] * twice(row_scale)
    codes_out[...] = PROTOS * assigned
    logit_grad = (PROTOS * (p_buf[z] * twice(prob_scale) - assigned)).astype(BF16)
    grad_proto = dot(unit_b, logit_grad, TN)
    proto = pr[...].astype(F32)
    col_norm = jnp.sqrt(jnp.sum(proto * proto, axis=0, keepdims=True) + NORM_EPS)
    unit_proto = proto / col_norm
    proto_out[...] = (
        grad_proto - unit_proto * jnp.sum(unit_proto * grad_proto, axis=0, keepdims=True)
    ) / col_norm

    side_out.landed()
    part = pl.ds(pl.multiple_of(lax.rem(clip * SHARE, LANES), SHARE), SHARE)

    def features(row):
        tall = jnp.concatenate([side_recv[:, row(b), :] for b in range(PAIR)], axis=0).T
        side_tmp[:, :CLIPS] = tall
        return side_tmp[part, :][:, :CLIPS]

    pooled_all = features(lambda b: b).astype(BF16)
    parts = []
    for head in range(PAIR):
        mix_all = features(lambda b: 2 + PAIR * b + head)
        high = mix_all.astype(BF16)
        parts += [high, (mix_all - high.astype(F32)).astype(BF16)]
    mix_parts = jnp.concatenate(parts, axis=0)

    gz_out.landed()
    grad_z = gz_recv[...].reshape(CLIPS, BOT).astype(BF16)
    proj_out[...] = dot(pooled_all, grad_z, NN)
    grad_pooled = dot(grad_z, wp[pl.ds(pl.multiple_of(cam * LANES, LANES), LANES), :], NT).astype(BF16)
    by_head = dot(mix_parts, grad_pooled, NN)
    lane = lax.broadcasted_iota(jnp.int32, (SHARE, LANES), 1)
    value_out[...] = jnp.where(
        lane < HD,
        by_head[:SHARE] + by_head[SHARE : 2 * SHARE],
        by_head[2 * SHARE : 3 * SHARE] + by_head[3 * SHARE :],
    )

    for out in [mix_out, gz_out, z_out, side_out, gs_out, gu_out] + row_out:
        out.left()


def finish(codes, proto_grad, proj_grad, value_grad, codes_out, proto_out, proj_out, value_out, order):
    for j in range(COLS // LANES):
        columns = slice(j * LANES, (j + 1) * LANES)
        for b in range(PAIR):
            order[j, pl.ds(b, N_CLIP, stride=PAIR), :] = codes[b * N_CLIP : (b + 1) * N_CLIP, columns]
        codes_out[:, columns] = order[j]
    proto_out[...] = proto_grad[...]
    proj_out[...] = proj_grad[...]
    value_out[...] = value_grad[...]


def local(tokens, w_query, w_key, w_value, w_proj, prototypes):
    vmem, dma = pltpu.VMEM, pltpu.SemaphoreType.DMA
    shapes = (
        jax.ShapeDtypeStruct((CLIPS, COLS), F32),
        jax.ShapeDtypeStruct((BOT, COLS), F32),
        jax.ShapeDtypeStruct((SHARE, BOT), F32),
        jax.ShapeDtypeStruct((SHARE, LANES), F32),
    )
    got = pl.pallas_call(
        kernel,
        out_shape=shapes,
        in_specs=[pl.BlockSpec(memory_space=pl.ANY)] * 6,
        out_specs=[pl.BlockSpec(memory_space=pltpu.VMEM)] * 4,
        scratch_shapes=[
            vmem((PAIR * TOK, D), BF16), vmem((D, D), BF16), vmem((D, D), BF16), vmem((D, D), BF16),
            vmem((D, BOT), BF16), vmem((BOT, COLS), BF16),
            vmem((N_Z, BOT, COLS), BF16),
            vmem((PAIR, N_CAM, TOK, LANES), BF16), vmem((PAIR, N_CAM, TOK, LANES), BF16),
            vmem((PAIR, N_CAM, PIECES, PIECE, LANES), BF16), vmem((PAIR, PIECES, N_CAM, PIECE, LANES), BF16),
            vmem((PAIR * PAIR, 8, KEYS), F32),
            vmem((N_CAM, 8, TOK), F32), vmem((N_CAM, 8, TOK), F32),
            vmem((N_CAM, PAIR * PAIR, D), F32), vmem((N_CAM, PAIR * PAIR, D), F32),
            vmem((PAIR * N_CAM, LANES), F32), vmem((N_CAM, PAIR * N_CAM, LANES), F32),
            vmem((4, LANES), F32), vmem((N_CLIP, 4, LANES), F32),
            vmem((N_CAM, 8, LANES), F32), vmem((N_CLIP, 8, LANES), F32),
            vmem((N_Z, CLIPS, COLS), F32), vmem((N_Z, CLIPS, COLS), F32),
            vmem((CLIPS, BOT), F32), vmem((CLIPS, BOT), F32), vmem((CLIPS, LANES), F32), vmem((CLIPS, LANES), F32),
            vmem((3, 1, LANES), F32), vmem((3, N_R, 1, LANES), F32),
            vmem((N_CAM, 8, BOT), F32), vmem((N_R, 8, BOT), F32),
            vmem((N_CAM, 8, BOT), F32), vmem((N_R, 8, BOT), F32),
            vmem((8, BOT), F32), vmem((N_CAM, 8, BOT), F32),
            vmem((LANES, LANES), F32),
            dma((7,)), dma((PAIR, PIECES + 1)), pltpu.SemaphoreType.REGULAR,
            dma((PAIR, PIECES + 1, N_CAM)), dma((PAIR, PIECES + 1, N_CAM)), dma((4,)), dma((4,)),
            dma((N_Z,)), dma((N_Z,)), dma((7,)), dma((7,)),
        ],
        compiler_params=pltpu.CompilerParams(
            collective_id=0, has_side_effects=True, vmem_limit_bytes=VMEM_LIMIT
        ),
    )(tokens.reshape(PAIR * TOK, D), w_query, w_key, w_value, w_proj, prototypes)
    return pl.pallas_call(
        finish,
        out_shape=shapes,
        in_specs=[pl.BlockSpec(memory_space=pltpu.VMEM)] * 4,
        out_specs=[pl.BlockSpec(memory_space=pltpu.VMEM)] * 4,
        scratch_shapes=[vmem((COLS // LANES, CLIPS, LANES), F32)],
    )(*got)


def solution(mesh):
    assert mesh.shape["cam"] == N_CAM and mesh.shape["clip"] == N_CLIP
    in_specs = (P("clip", "cam", None, None), P(), P(), P(), P(), P(None, ("cam", "clip")))
    out_specs = (
        P(None, ("cam", "clip")),
        P(None, ("cam", "clip")),
        P("clip", None),
        P("clip", "cam"),
    )
    return jax.shard_map(local, mesh=mesh, in_specs=in_specs, out_specs=out_specs, check_vma=False)
```

```python
import functools

import jax
import jax.numpy as jnp
from jax import lax
from jax.experimental import pallas as pl
from jax.experimental.pallas import tpu as pltpu
from jax.sharding import PartitionSpec as P

D = 1024
HD = 64
H = 16
BOT = 256
PROTOS = 65536
TOK = 256
CLIPS = 64
N_CAM = 8
N_CLIP = 32
N_Z = 8
N_Y = N_CLIP // N_Z
N_R = N_CAM * N_Y
PAIR = 2
LANES = 128
COLS = PROTOS // (N_CAM * N_CLIP)
SHARE = D // N_CLIP
KEYS = N_CAM * TOK
PIECES = 2
PIECE = TOK // PIECES
ROWS = N_CAM * PIECE

VMEM_LIMIT = 58 * 2**20

SINK_EPS = 0.05
SOFTMAX_TEMP = 0.1
NORM_EPS = 1e-06
LOG2_E = 1.4426950408889634

MESH = pl.DeviceIdType.MESH
F32 = jnp.float32
BF16 = jnp.bfloat16


CAM_ORDER = (4, 6, 2, 5, 3, 7, 1)
Y_ORDER = (2, 1, 3, 0)
Z_ORDER = (4, 3, 5, 2, 6, 1, 7, 0)
CLIP_ORDER = tuple((oy, oz) for oy in Y_ORDER for oz in Z_ORDER if (oy, oz) != (0, 0))
R_ORDER = tuple((oy, oc) for oy in Y_ORDER for oc in CAM_ORDER + (0,) if (oy, oc) != (0, 0))


def dot(a, b, dims):
    return lax.dot_general(a, b, (dims, ((), ())), preferred_element_type=F32)


NN = ((1,), (0,))
NT = ((1,), (1,))
TN = ((0,), (0,))


def split_dot(a, b):
    high = a.astype(BF16)
    low = (a - high.astype(F32)).astype(BF16)
    got = dot(jnp.concatenate([high, low], axis=0), b, NT)
    return got[: a.shape[0]] + got[a.shape[0] :]


def fold(a):
    return a[:, :LANES] + a[:, LANES:]


def twice(a):
    return jnp.concatenate([a, a], axis=1)


def kernel(
    x_in, wq_in, wk_in, wv_in, wp_in, pr_in,
    codes_out, proto_out, proj_out, value_out,
    xv, wq, wk, wv, wp, pr,
    proto_all, k_send, k_recv, q_send, q_recv, acc,
    w_send, w_recv, mix_send, mix_recv, pool_send, pool_recv,
    z_send, z_recv, side_send, side_recv,
    a_buf, p_buf, unit_buf, norm_buf, prob_buf, scale_buf,
    row_send, row_recv, gs_send, gs_recv, gu_send, gu_recv, gz_send, gz_recv,
    side_tmp,
    load_sem, own_sem, y_sem, qk_ss, qk_rs, cam_ss, cam_rs, proto_ss, proto_rs, wide_ss, wide_rs,
):
    cam = lax.axis_index("cam")
    clip = lax.axis_index("clip")
    y, z = lax.div(clip, N_Z), lax.rem(clip, N_Z)
    here = y * N_CAM + cam

    cams = [cam] + [lax.rem(cam + o, N_CAM) for o in range(1, N_CAM)]
    lines = [lax.rem(y + o, N_Y) * N_Z for o in range(N_Y)]
    depths = [z] + [lax.rem(z + o, N_Z) for o in range(1, N_Z)]

    def cam_peer(o):
        return (cams[o], clip)

    def yz_peer(oy, oz):
        return (cam, lines[oy] + depths[oz])

    def r_peer(oy, oc):
        return (cams[oc], lines[oy] + z)

    def loop(lo, hi, step):
        def body(i, carry):
            step(i)
            return carry

        lax.fori_loop(lo, hi, body, 0)

    barrier = pltpu.get_barrier_semaphore()
    for oz in Z_ORDER[:-1]:
        pl.semaphore_signal(barrier, inc=1, device_id=yz_peer(0, oz), device_id_type=MESH)
    for oy in Y_ORDER[:-1]:
        pl.semaphore_signal(barrier, inc=1, device_id=yz_peer(oy, 0), device_id_type=MESH)
    for o in CAM_ORDER:
        pl.semaphore_signal(barrier, inc=1, device_id=cam_peer(o), device_id_type=MESH)

    loads = [
        pltpu.make_async_copy(x_in.at[pl.ds(0, TOK)], xv.at[pl.ds(0, TOK)], load_sem.at[0]),
        pltpu.make_async_copy(wk_in, wk, load_sem.at[1]),
        pltpu.make_async_copy(wq_in, wq, load_sem.at[2]),
        pltpu.make_async_copy(x_in.at[pl.ds(TOK, TOK)], xv.at[pl.ds(TOK, TOK)], load_sem.at[3]),
        pltpu.make_async_copy(pr_in, pr, load_sem.at[4]),
        pltpu.make_async_copy(wv_in, wv, load_sem.at[5]),
        pltpu.make_async_copy(wp_in, wp, load_sem.at[6]),
    ]
    for load in loads[:2]:
        load.start()

    def project_keys(b):
        rows = xv[b * TOK : (b + 1) * TOK, :]
        for j in range(D // 256):
            got = dot(rows, wk[:, j * 256 : (j + 1) * 256], NN).astype(BF16)
            k_send[b, 2 * j] = got[:, :LANES]
            k_send[b, 2 * j + 1] = got[:, LANES:]

    def project_queries(b):
        rows = xv[b * TOK : (b + 1) * TOK, :]
        for j in range(D // 256):
            got = dot(rows, wq[:, j * 256 : (j + 1) * 256], NN).astype(BF16)
            q_send[b, 2 * j] = got[:, :LANES].reshape(PIECES, PIECE, LANES)
            q_send[b, 2 * j + 1] = got[:, LANES:].reshape(PIECES, PIECE, LANES)

    def remote(src, dst, send_sem, recv_sem, to):
        return pltpu.make_async_remote_copy(
            src_ref=src, dst_ref=dst, send_sem=send_sem, recv_sem=recv_sem,
            device_id=to, device_id_type=MESH,
        )

    def k_copy(b, o):
        to = cam_peer(o)
        return remote(k_send.at[b, to[0]], k_recv.at[b, cam], qk_ss.at[b, PIECES, o], qk_rs.at[b, PIECES, o], to)

    def q_copy(b, part, o):
        to = cam_peer(o)
        return remote(
            q_send.at[b, to[0], part], q_recv.at[b, part, cam], qk_ss.at[b, part, o], qk_rs.at[b, part, o], to
        )

    def own_k(b):
        return pltpu.make_async_copy(k_send.at[b, cam], k_recv.at[b, cam], own_sem.at[b, PIECES])

    def own_q(b, part):
        return pltpu.make_async_copy(q_send.at[b, cam, part], q_recv.at[b, part, cam], own_sem.at[b, part])

    def send_keys(b):
        for o in CAM_ORDER:
            k_copy(b, o).start()
        own_k(b).start()

    def send_queries(b):
        for part in range(PIECES):
            for o in CAM_ORDER:
                q_copy(b, part, o).start()
            own_q(b, part).start()

    def proto_copy(i):
        return remote(proto_all.at[z], proto_all.at[z], proto_ss.at[i], proto_rs.at[i], yz_peer(0, Z_ORDER[i]))

    loads[0].wait()
    loads[1].wait()
    for load in loads[2:]:
        load.start()
    project_keys(0)
    pl.semaphore_wait(barrier, N_CAM - 1 + N_Y - 1 + N_Z - 1)
    send_keys(0)
    for oy in Y_ORDER[:-1]:
        pl.semaphore_signal(y_sem, inc=1, device_id=yz_peer(oy, 0), device_id_type=MESH)
    loads[2].wait()
    project_queries(0)
    send_queries(0)
    loads[3].wait()
    project_keys(1)
    send_keys(1)
    project_queries(1)
    send_queries(1)

    loads[4].wait()
    proto = pr[...].astype(F32)
    col_norm = jnp.sqrt(jnp.sum(proto * proto, axis=0, keepdims=True) + NORM_EPS)
    proto_all[z] = (proto / col_norm).astype(BF16)
    for i in range(N_Z - 1):
        proto_copy(i).start()

    acc[...] = jnp.zeros_like(acc)
    lane_q = lax.broadcasted_iota(jnp.int32, (ROWS, LANES), 1)

    def attend(b):
        for o in CAM_ORDER[::-1]:
            k_copy(b, o).wait_recv()
        own_k(b).wait()

        def piece(part):
            for o in CAM_ORDER[::-1]:
                q_copy(b, part, o).wait_recv()
            own_q(b, part).wait()
            keys = k_recv[b].reshape(KEYS, LANES)
            both = q_recv[b, part].reshape(ROWS, LANES)
            for head in range(PAIR):
                rows = jnp.where((lane_q < HD) == (head == 0), both, jnp.zeros_like(both))
                weights = jnp.exp2(dot(rows, keys, NT) * (HD ** (-0.5) * LOG2_E))
                weights = weights * (1.0 / jnp.sum(weights, axis=1, keepdims=True))
                acc[b * PAIR + head] += jnp.sum(weights.reshape(ROWS // 8, 8, KEYS), axis=0)

        loop(0, PIECES, piece)

    loop(0, PAIR, attend)

    class Exchange:
        def __init__(self, order, peer, src, slots, mine, send_sem, recv_sem):
            self.order, self.peer, self.src, self.dst = order, peer, src, slots.at[mine]
            self.send_sem, self.recv_sem = send_sem, recv_sem
            others = slots.at[pl.ds(0, len(order))]
            self.whole = remote(others, others, send_sem, recv_sem, peer(order[0]))

        def start(self):
            for o in self.order:
                to = self.peer(o)
                remote(self.src(to), self.dst, self.send_sem, self.recv_sem, to).start()

        def landed(self):
            self.whole.wait_recv()

        def left(self):
            self.whole.wait_send()

    def cam_exchange(k, src, slots):
        return Exchange(CAM_ORDER, cam_peer, src, slots, cam, cam_ss.at[k], cam_rs.at[k])

    def clip_exchange(k, src, slots):
        return Exchange(CLIP_ORDER, lambda o: yz_peer(*o), src, slots, clip, wide_ss.at[k], wide_rs.at[k])

    def r_exchange(k, src, slots):
        return Exchange(R_ORDER, lambda o: r_peer(*o), src, slots, here, wide_ss.at[k], wide_rs.at[k])

    w_out = cam_exchange(0, lambda to: w_send.at[to[0]], w_recv)
    pool_out = cam_exchange(1, lambda to: pool_send, pool_recv)
    mix_out = cam_exchange(2, lambda to: mix_send.at[to[0]], mix_recv)
    gz_out = cam_exchange(3, lambda to: gz_send, gz_recv)
    z_out = clip_exchange(0, lambda to: z_send, z_recv)
    side_out = clip_exchange(1, lambda to: side_send.at[lax.div(to[1] * SHARE, LANES)], side_recv)
    gu_out = r_exchange(2, lambda to: gu_send.at[to[0]], gu_recv)
    gs_out = r_exchange(6, lambda to: gs_send.at[to[0]], gs_recv)

    def row_exchange(step):
        return r_exchange(3 + step, lambda to: row_send.at[step], row_recv.at[step])

    row_out = [row_exchange(step) for step in range(3)]

    row8 = lax.broadcasted_iota(jnp.int32, (8, KEYS), 0)
    weights = jnp.zeros((8, KEYS), F32)
    for r in range(PAIR * PAIR):
        weights = jnp.where(row8 == r, jnp.sum(acc[r], axis=0, keepdims=True) * (1.0 / KEYS), weights)
    for p in range(N_CAM):
        w_send[p] = weights[:, p * TOK : (p + 1) * TOK]
    w_out.start()
    w_recv[cam] = w_send[cam]
    loads[5].wait()
    w_out.landed()

    key_weight = w_recv[...].reshape(8 * N_CAM, TOK).astype(BF16)
    mix0 = dot(key_weight, xv[:TOK, :], NN)
    mix1 = dot(key_weight, xv[TOK:, :], NN)
    row64 = lax.broadcasted_iota(jnp.int32, (8 * N_CAM, D), 0)
    mixture = jnp.where(lax.rem(row64, 8) >= PAIR, mix1, mix0).astype(BF16)
    head_out = dot(mixture, wv[...], NN)
    lane8 = lax.broadcasted_iota(jnp.int32, (8, LANES), 1)
    sub8 = lax.broadcasted_iota(jnp.int32, (8, LANES), 0)
    own_head = lax.rem(sub8, PAIR) == lax.div(lane8, HD)
    for p in range(N_CAM):
        tile = head_out[p * 8 : (p + 1) * 8, p * LANES : (p + 1) * LANES]
        tile = jnp.where(own_head, tile, 0.0)
        pool_send[p : p + 1, :] = tile[0:1] + tile[1:2]
        pool_send[N_CAM + p : N_CAM + p + 1, :] = tile[2:3] + tile[3:4]
    pool_out.start()
    pool_recv[cam] = pool_send[...]
    mixture_f = mixture.astype(F32)
    for p in range(N_CAM):
        mix_send[p] = mixture_f[p * 8 : p * 8 + PAIR * PAIR, :]
    mix_out.start()
    mix_recv[cam] = mix_send[cam]
    loads[6].wait()
    pool_out.landed()
    pooled = jnp.sum(pool_recv[...], axis=0).astype(BF16)
    row16 = lax.broadcasted_iota(jnp.int32, (PAIR * N_CAM, LANES), 0)
    spread = jnp.concatenate(
        [jnp.where(lax.rem(row16, N_CAM) == p, pooled, jnp.zeros_like(pooled)) for p in range(N_CAM)], axis=1
    )
    z_rows = dot(spread, wp[...], NN)
    for b in range(PAIR):
        z_clip = jnp.sum(z_rows[b * N_CAM : (b + 1) * N_CAM], axis=0, keepdims=True)
        for j in range(2):
            z_send[2 * b + j : 2 * b + j + 1, :] = z_clip[:, j * LANES : (j + 1) * LANES]
    pl.semaphore_wait(y_sem, N_Y - 1)
    z_out.start()
    z_recv[clip] = z_send[...]

    def left(b):
        for o in CAM_ORDER:
            k_copy(b, o).wait_send()

        def part_left(part):
            for o in CAM_ORDER:
                q_copy(b, part, o).wait_send()

        loop(0, PIECES, part_left)

    loop(0, PAIR, left)
    for i in range(N_Z - 1):
        proto_copy(i).wait_send()
    w_out.left()
    pool_out.left()

    mix_out.landed()
    mix_sum = jnp.sum(mix_recv[...], axis=0)
    pooled_f = pooled.astype(F32)
    for p in range(N_CAM):
        side_send[p, 0:1, :] = pooled_f[p : p + 1]
        side_send[p, 1:2, :] = pooled_f[N_CAM + p : N_CAM + p + 1]
        side_send[p, 2:6, :] = mix_sum[:, p * LANES : (p + 1) * LANES]
        side_send[p, 6:8, :] = jnp.zeros((2, LANES), F32)
    for i in range(N_Z - 1):
        proto_copy(i).wait_recv()
    z_out.landed()

    embed = jnp.concatenate(
        [jnp.concatenate([z_recv[:, 2 * b + j, :] for j in range(2)], axis=1) for b in range(PAIR)], axis=0
    )
    norm = jnp.sqrt(jnp.sum(embed * embed, axis=1, keepdims=True) + NORM_EPS)
    unit = embed / norm
    unit_buf[...] = unit
    norm_buf[...] = jnp.broadcast_to(norm, norm_buf.shape)
    unit_b = unit.astype(BF16)

    def total(step, sums, meanwhile=None):
        tall = jnp.broadcast_to(jnp.sum(sums, axis=1, keepdims=True), (LANES, LANES))
        row_send[step] = tall.T[:1, :]
        row_out[step].start()
        row_recv[step, here] = row_send[step]
        if meanwhile is not None:
            meanwhile()
        row_out[step].landed()
        wide = jnp.sum(row_recv[step], axis=0)
        return jnp.broadcast_to(wide, (LANES, LANES)).T

    zero = jnp.zeros((CLIPS, LANES), F32)

    def first(s, carry):
        rows, probs = carry
        exps = jnp.exp(dot(unit_b, proto_all[s], NN) * (1.0 / SOFTMAX_TEMP))
        scores = exps * exps
        p_buf[s] = exps
        a_buf[s] = scores
        scaled = scores * (1.0 / jnp.sum(scores, axis=0, keepdims=True))
        return rows + fold(scaled), probs + fold(exps)

    rows, probs = lax.fori_loop(0, N_Z, first, (zero, zero), unroll=True)

    def spread_rows(send, out, recv, value):
        for p in range(N_CAM):
            send[p] = value[p * 8 : (p + 1) * 8]
        out.start()
        recv[here] = send[cam]

    empty = jnp.zeros((CLIPS, BOT), F32)

    def while_waiting():
        side_out.start()
        side_recv[clip] = side_send[lax.div(clip * SHARE, LANES)]
        soft = lax.fori_loop(0, N_Z, lambda s, sums: sums + split_dot(p_buf[s], proto_all[s]), empty, unroll=True)
        spread_rows(gs_send, gs_out, gs_recv, soft)

    got = total(0, jnp.concatenate([rows, probs], axis=0), while_waiting)
    row_scale = 1.0 / got[:CLIPS]
    prob_scale = 1.0 / got[CLIPS:]
    prob_buf[...] = prob_scale

    def rescale(s, wide_scale):
        scores = a_buf[s]
        return scores * (1.0 / jnp.sum(scores * wide_scale, axis=0, keepdims=True))

    wide_scale = twice(row_scale)
    rows = lax.fori_loop(0, N_Z, lambda s, sums: sums + fold(rescale(s, wide_scale)), zero, unroll=True)
    row_scale = 1.0 / total(1, jnp.concatenate([rows, rows], axis=0))[:CLIPS]
    last_scale = twice(row_scale)

    def last(s, carry):
        rows, sums = carry
        scaled = rescale(s, last_scale)
        a_buf[s] = scaled
        return rows + fold(scaled), sums + split_dot(scaled, proto_all[s])

    rows, hard = lax.fori_loop(0, N_Z, last, (zero, empty), unroll=True)
    spread_rows(gu_send, gu_out, gu_recv, hard)
    row_scale = 1.0 / total(2, jnp.concatenate([rows, rows], axis=0))[:CLIPS]
    scale_buf[...] = row_scale

    mine = pl.ds(pl.multiple_of(cam * 8, 8), 8)
    gs_out.landed()
    grad8 = jnp.sum(gs_recv[...], axis=0) * twice(prob_buf[mine, :])
    gu_out.landed()
    grad8 = PROTOS * (grad8 - jnp.sum(gu_recv[...], axis=0) * twice(scale_buf[mine, :]))
    unit8 = unit_buf[mine, :]
    grad8 = (grad8 - unit8 * jnp.sum(unit8 * grad8, axis=1, keepdims=True)) / norm_buf[mine, :]
    gz_send[...] = grad8.astype(BF16).astype(F32)
    gz_out.start()
    gz_recv[cam] = gz_send[...]

    assigned = a_buf[z] * twice(row_scale)
    codes_out[...] = PROTOS * assigned
    logit_grad = (PROTOS * (p_buf[z] * twice(prob_scale) - assigned)).astype(BF16)
    grad_proto = dot(unit_b, logit_grad, TN)
    proto = pr[...].astype(F32)
    col_norm = jnp.sqrt(jnp.sum(proto * proto, axis=0, keepdims=True) + NORM_EPS)
    unit_proto = proto / col_norm
    proto_out[...] = (
        grad_proto - unit_proto * jnp.sum(unit_proto * grad_proto, axis=0, keepdims=True)
    ) / col_norm

    side_out.landed()
    part = pl.ds(pl.multiple_of(lax.rem(clip * SHARE, LANES), SHARE), SHARE)

    def features(row):
        tall = jnp.concatenate([side_recv[:, row(b), :] for b in range(PAIR)], axis=0).T
        side_tmp[:, :CLIPS] = tall
        return side_tmp[part, :][:, :CLIPS]

    pooled_all = features(lambda b: b).astype(BF16)
    parts = []
    for head in range(PAIR):
        mix_all = features(lambda b: 2 + PAIR * b + head)
        high = mix_all.astype(BF16)
        parts += [high, (mix_all - high.astype(F32)).astype(BF16)]
    mix_parts = jnp.concatenate(parts, axis=0)

    gz_out.landed()
    grad_z = gz_recv[...].reshape(CLIPS, BOT).astype(BF16)
    proj_out[...] = dot(pooled_all, grad_z, NN)
    grad_pooled = dot(grad_z, wp[pl.ds(pl.multiple_of(cam * LANES, LANES), LANES), :], NT).astype(BF16)
    by_head = dot(mix_parts, grad_pooled, NN)
    lane = lax.broadcasted_iota(jnp.int32, (SHARE, LANES), 1)
    value_out[...] = jnp.where(
        lane < HD,
        by_head[:SHARE] + by_head[SHARE : 2 * SHARE],
        by_head[2 * SHARE : 3 * SHARE] + by_head[3 * SHARE :],
    )

    for out in [mix_out, gz_out, z_out, side_out, gs_out, gu_out] + row_out:
        out.left()


def finish(codes, proto_grad, proj_grad, value_grad, codes_out, proto_out, proj_out, value_out, order):
    for j in range(COLS // LANES):
        columns = slice(j * LANES, (j + 1) * LANES)
        for b in range(PAIR):
            order[j, pl.ds(b, N_CLIP, stride=PAIR), :] = codes[b * N_CLIP : (b + 1) * N_CLIP, columns]
        codes_out[:, columns] = order[j]
    proto_out[...] = proto_grad[...]
    proj_out[...] = proj_grad[...]
    value_out[...] = value_grad[...]


def local(tokens, w_query, w_key, w_value, w_proj, prototypes):
    vmem, dma = pltpu.VMEM, pltpu.SemaphoreType.DMA
    shapes = (
        jax.ShapeDtypeStruct((CLIPS, COLS), F32),
        jax.ShapeDtypeStruct((BOT, COLS), F32),
        jax.ShapeDtypeStruct((SHARE, BOT), F32),
        jax.ShapeDtypeStruct((SHARE, LANES), F32),
    )
    got = pl.pallas_call(
        kernel,
        out_shape=shapes,
        in_specs=[pl.BlockSpec(memory_space=pl.ANY)] * 6,
        out_specs=[pl.BlockSpec(memory_space=pltpu.VMEM)] * 4,
        scratch_shapes=[
            vmem((PAIR * TOK, D), BF16), vmem((D, D), BF16), vmem((D, D), BF16), vmem((D, D), BF16),
            vmem((D, BOT), BF16), vmem((BOT, COLS), BF16),
            vmem((N_Z, BOT, COLS), BF16),
            vmem((PAIR, N_CAM, TOK, LANES), BF16), vmem((PAIR, N_CAM, TOK, LANES), BF16),
            vmem((PAIR, N_CAM, PIECES, PIECE, LANES), BF16), vmem((PAIR, PIECES, N_CAM, PIECE, LANES), BF16),
            vmem((PAIR * PAIR, 8, KEYS), F32),
            vmem((N_CAM, 8, TOK), F32), vmem((N_CAM, 8, TOK), F32),
            vmem((N_CAM, PAIR * PAIR, D), F32), vmem((N_CAM, PAIR * PAIR, D), F32),
            vmem((PAIR * N_CAM, LANES), F32), vmem((N_CAM, PAIR * N_CAM, LANES), F32),
            vmem((4, LANES), F32), vmem((N_CLIP, 4, LANES), F32),
            vmem((N_CAM, 8, LANES), F32), vmem((N_CLIP, 8, LANES), F32),
            vmem((N_Z, CLIPS, COLS), F32), vmem((N_Z, CLIPS, COLS), F32),
            vmem((CLIPS, BOT), F32), vmem((CLIPS, BOT), F32), vmem((CLIPS, LANES), F32), vmem((CLIPS, LANES), F32),
            vmem((3, 1, LANES), F32), vmem((3, N_R, 1, LANES), F32),
            vmem((N_CAM, 8, BOT), F32), vmem((N_R, 8, BOT), F32),
            vmem((N_CAM, 8, BOT), F32), vmem((N_R, 8, BOT), F32),
            vmem((8, BOT), F32), vmem((N_CAM, 8, BOT), F32),
            vmem((LANES, LANES), F32),
            dma((7,)), dma((PAIR, PIECES + 1)), pltpu.SemaphoreType.REGULAR,
            dma((PAIR, PIECES + 1, N_CAM)), dma((PAIR, PIECES + 1, N_CAM)), dma((4,)), dma((4,)),
            dma((N_Z,)), dma((N_Z,)), dma((7,)), dma((7,)),
        ],
        compiler_params=pltpu.CompilerParams(
            collective_id=0, has_side_effects=True, vmem_limit_bytes=VMEM_LIMIT
        ),
    )(tokens.reshape(PAIR * TOK, D), w_query, w_key, w_value, w_proj, prototypes)
    return pl.pallas_call(
        finish,
        out_shape=shapes,
        in_specs=[pl.BlockSpec(memory_space=pltpu.VMEM)] * 4,
        out_specs=[pl.BlockSpec(memory_space=pltpu.VMEM)] * 4,
        scratch_shapes=[vmem((COLS // LANES, CLIPS, LANES), F32)],
    )(*got)


def solution(mesh):
    assert mesh.shape["cam"] == N_CAM and mesh.shape["clip"] == N_CLIP
    in_specs = (P("clip", "cam", None, None), P(), P(), P(), P(), P(None, ("cam", "clip")))
    out_specs = (
        P(None, ("cam", "clip")),
        P(None, ("cam", "clip")),
        P("clip", None),
        P("clip", "cam"),
    )
    return jax.shard_map(local, mesh=mesh, in_specs=in_specs, out_specs=out_specs, check_vma=False)
```

```python
import functools

import jax
import jax.numpy as jnp
from jax import lax
from jax.experimental import pallas as pl
from jax.experimental.pallas import tpu as pltpu
from jax.sharding import PartitionSpec as P

D = 1024
HD = 64
H = 16
BOT = 256
PROTOS = 65536
TOK = 256
CLIPS = 64
N_CAM = 8
N_CLIP = 32
N_Z = 8
N_Y = N_CLIP // N_Z
N_R = N_CAM * N_Y
PAIR = 2
LANES = 128
COLS = PROTOS // (N_CAM * N_CLIP)
SHARE = D // N_CLIP
KEYS = N_CAM * TOK
PIECES = 4
PIECE = TOK // PIECES
ROWS = N_CAM * PIECE

VMEM_LIMIT = 58 * 2**20

SINK_EPS = 0.05
SOFTMAX_TEMP = 0.1
NORM_EPS = 1e-06
LOG2_E = 1.4426950408889634

MESH = pl.DeviceIdType.MESH
F32 = jnp.float32
BF16 = jnp.bfloat16


CAM_ORDER = (4, 6, 2, 5, 3, 7, 1)
Y_ORDER = (2, 1, 3, 0)
Z_ORDER = (4, 3, 5, 2, 6, 1, 7, 0)
CLIP_ORDER = tuple((oy, oz) for oy in Y_ORDER for oz in Z_ORDER if (oy, oz) != (0, 0))
R_ORDER = tuple((oy, oc) for oy in Y_ORDER for oc in CAM_ORDER + (0,) if (oy, oc) != (0, 0))


def dot(a, b, dims):
    return lax.dot_general(a, b, (dims, ((), ())), preferred_element_type=F32)


NN = ((1,), (0,))
NT = ((1,), (1,))
TN = ((0,), (0,))


def split_dot(a, b):
    high = a.astype(BF16)
    low = (a - high.astype(F32)).astype(BF16)
    got = dot(jnp.concatenate([high, low], axis=0), b, NT)
    return got[: a.shape[0]] + got[a.shape[0] :]


def fold(a):
    return a[:, :LANES] + a[:, LANES:]


def twice(a):
    return jnp.concatenate([a, a], axis=1)


def kernel(
    x_in, wq_in, wk_in, wv_in, wp_in, pr_in,
    codes_out, proto_out, proj_out, value_out,
    xv, wq, wk, wv, wp, pr,
    proto_all, k_send, k_recv, q_send, q_recv, acc,
    w_send, w_recv, mix_send, mix_recv, pool_send, pool_recv,
    z_send, z_recv, side_send, side_recv,
    a_buf, p_buf, unit_buf, norm_buf, prob_buf, scale_buf,
    row_send, row_recv, gs_send, gs_recv, gu_send, gu_recv, gz_send, gz_recv,
    side_tmp,
    load_sem, own_sem, y_sem, qk_ss, qk_rs, cam_ss, cam_rs, proto_ss, proto_rs, wide_ss, wide_rs,
):
    cam = lax.axis_index("cam")
    clip = lax.axis_index("clip")
    y, z = lax.div(clip, N_Z), lax.rem(clip, N_Z)
    here = y * N_CAM + cam

    cams = [cam] + [lax.rem(cam + o, N_CAM) for o in range(1, N_CAM)]
    lines = [lax.rem(y + o, N_Y) * N_Z for o in range(N_Y)]
    depths = [z] + [lax.rem(z + o, N_Z) for o in range(1, N_Z)]

    def cam_peer(o):
        return (cams[o], clip)

    def yz_peer(oy, oz):
        return (cam, lines[oy] + depths[oz])

    def r_peer(oy, oc):
        return (cams[oc], lines[oy] + z)

    def loop(lo, hi, step):
        def body(i, carry):
            step(i)
            return carry

        lax.fori_loop(lo, hi, body, 0)

    barrier = pltpu.get_barrier_semaphore()
    for oz in Z_ORDER[:-1]:
        pl.semaphore_signal(barrier, inc=1, device_id=yz_peer(0, oz), device_id_type=MESH)
    for oy in Y_ORDER[:-1]:
        pl.semaphore_signal(barrier, inc=1, device_id=yz_peer(oy, 0), device_id_type=MESH)
    for o in CAM_ORDER:
        pl.semaphore_signal(barrier, inc=1, device_id=cam_peer(o), device_id_type=MESH)

    loads = [
        pltpu.make_async_copy(x_in.at[pl.ds(0, TOK)], xv.at[pl.ds(0, TOK)], load_sem.at[0]),
        pltpu.make_async_copy(wk_in, wk, load_sem.at[1]),
        pltpu.make_async_copy(wq_in, wq, load_sem.at[2]),
        pltpu.make_async_copy(x_in.at[pl.ds(TOK, TOK)], xv.at[pl.ds(TOK, TOK)], load_sem.at[3]),
        pltpu.make_async_copy(pr_in, pr, load_sem.at[4]),
        pltpu.make_async_copy(wv_in, wv, load_sem.at[5]),
        pltpu.make_async_copy(wp_in, wp, load_sem.at[6]),
    ]
    for load in loads[:2]:
        load.start()

    def project_keys(b):
        rows = xv[b * TOK : (b + 1) * TOK, :]
        for j in range(D // 256):
            got = dot(rows, wk[:, j * 256 : (j + 1) * 256], NN).astype(BF16)
            k_send[b, 2 * j] = got[:, :LANES]
            k_send[b, 2 * j + 1] = got[:, LANES:]

    def project_queries(b):
        rows = xv[b * TOK : (b + 1) * TOK, :]
        for j in range(D // 256):
            got = dot(rows, wq[:, j * 256 : (j + 1) * 256], NN).astype(BF16)
            q_send[b, 2 * j] = got[:, :LANES].reshape(PIECES, PIECE, LANES)
            q_send[b, 2 * j + 1] = got[:, LANES:].reshape(PIECES, PIECE, LANES)

    def remote(src, dst, send_sem, recv_sem, to):
        return pltpu.make_async_remote_copy(
            src_ref=src, dst_ref=dst, send_sem=send_sem, recv_sem=recv_sem,
            device_id=to, device_id_type=MESH,
        )

    def k_copy(b, o):
        to = cam_peer(o)
        return remote(k_send.at[b, to[0]], k_recv.at[b, cam], qk_ss.at[b, PIECES, o], qk_rs.at[b, PIECES, o], to)

    def q_copy(b, part, o):
        to = cam_peer(o)
        return remote(
            q_send.at[b, to[0], part], q_recv.at[b, part, cam], qk_ss.at[b, part, o], qk_rs.at[b, part, o], to
        )

    def own_k(b):
        return pltpu.make_async_copy(k_send.at[b, cam], k_recv.at[b, cam], own_sem.at[b, PIECES])

    def own_q(b, part):
        return pltpu.make_async_copy(q_send.at[b, cam, part], q_recv.at[b, part, cam], own_sem.at[b, part])

    def send_keys(b):
        for o in CAM_ORDER:
            k_copy(b, o).start()
        own_k(b).start()

    def send_queries(b):
        for part in range(PIECES):
            for o in CAM_ORDER:
                q_copy(b, part, o).start()
            own_q(b, part).start()

    def proto_copy(i):
        return remote(proto_all.at[z], proto_all.at[z], proto_ss.at[i], proto_rs.at[i], yz_peer(0, Z_ORDER[i]))

    loads[0].wait()
    loads[1].wait()
    for load in loads[2:]:
        load.start()
    project_keys(0)
    pl.semaphore_wait(barrier, N_CAM - 1 + N_Y - 1 + N_Z - 1)
    send_keys(0)
    for oy in Y_ORDER[:-1]:
        pl.semaphore_signal(y_sem, inc=1, device_id=yz_peer(oy, 0), device_id_type=MESH)
    loads[2].wait()
    project_queries(0)
    send_queries(0)
    loads[3].wait()
    project_keys(1)
    send_keys(1)
    project_queries(1)
    send_queries(1)

    loads[4].wait()
    proto = pr[...].astype(F32)
    col_norm = jnp.sqrt(jnp.sum(proto * proto, axis=0, keepdims=True) + NORM_EPS)
    proto_all[z] = (proto / col_norm).astype(BF16)
    for i in range(N_Z - 1):
        proto_copy(i).start()

    acc[...] = jnp.zeros_like(acc)
    lane_q = lax.broadcasted_iota(jnp.int32, (ROWS, LANES), 1)

    def attend(b):
        for o in CAM_ORDER[::-1]:
            k_copy(b, o).wait_recv()
        own_k(b).wait()

        def piece(part):
            for o in CAM_ORDER[::-1]:
                q_copy(b, part, o).wait_recv()
            own_q(b, part).wait()
            keys = k_recv[b].reshape(KEYS, LANES)
            both = q_recv[b, part].reshape(ROWS, LANES)
            for head in range(PAIR):
                rows = jnp.where((lane_q < HD) == (head == 0), both, jnp.zeros_like(both))
                weights = jnp.exp2(dot(rows, keys, NT) * (HD ** (-0.5) * LOG2_E))
                weights = weights * (1.0 / jnp.sum(weights, axis=1, keepdims=True))
                acc[b * PAIR + head] += jnp.sum(weights.reshape(ROWS // 8, 8, KEYS), axis=0)

        loop(0, PIECES, piece)

    loop(0, PAIR, attend)

    class Exchange:
        def __init__(self, order, peer, src, slots, mine, send_sem, recv_sem):
            self.order, self.peer, self.src, self.dst = order, peer, src, slots.at[mine]
            self.send_sem, self.recv_sem = send_sem, recv_sem
            others = slots.at[pl.ds(0, len(order))]
            self.whole = remote(others, others, send_sem, recv_sem, peer(order[0]))

        def start(self):
            for o in self.order:
                to = self.peer(o)
                remote(self.src(to), self.dst, self.send_sem, self.recv_sem, to).start()

        def landed(self):
            self.whole.wait_recv()

        def left(self):
            self.whole.wait_send()

    def cam_exchange(k, src, slots):
        return Exchange(CAM_ORDER, cam_peer, src, slots, cam, cam_ss.at[k], cam_rs.at[k])

    def clip_exchange(k, src, slots):
        return Exchange(CLIP_ORDER, lambda o: yz_peer(*o), src, slots, clip, wide_ss.at[k], wide_rs.at[k])

    def r_exchange(k, src, slots):
        return Exchange(R_ORDER, lambda o: r_peer(*o), src, slots, here, wide_ss.at[k], wide_rs.at[k])

    w_out = cam_exchange(0, lambda to: w_send.at[to[0]], w_recv)
    pool_out = cam_exchange(1, lambda to: pool_send, pool_recv)
    mix_out = cam_exchange(2, lambda to: mix_send.at[to[0]], mix_recv)
    gz_out = cam_exchange(3, lambda to: gz_send, gz_recv)
    z_out = clip_exchange(0, lambda to: z_send, z_recv)
    side_out = clip_exchange(1, lambda to: side_send.at[lax.div(to[1] * SHARE, LANES)], side_recv)
    gu_out = r_exchange(2, lambda to: gu_send.at[to[0]], gu_recv)
    gs_out = r_exchange(6, lambda to: gs_send.at[to[0]], gs_recv)

    def row_exchange(step):
        return r_exchange(3 + step, lambda to: row_send.at[step], row_recv.at[step])

    row_out = [row_exchange(step) for step in range(3)]

    row8 = lax.broadcasted_iota(jnp.int32, (8, KEYS), 0)
    weights = jnp.zeros((8, KEYS), F32)
    for r in range(PAIR * PAIR):
        weights = jnp.where(row8 == r, jnp.sum(acc[r], axis=0, keepdims=True) * (1.0 / KEYS), weights)
    for p in range(N_CAM):
        w_send[p] = weights[:, p * TOK : (p + 1) * TOK]
    w_out.start()
    w_recv[cam] = w_send[cam]
    loads[5].wait()
    w_out.landed()

    key_weight = w_recv[...].reshape(8 * N_CAM, TOK).astype(BF16)
    mix0 = dot(key_weight, xv[:TOK, :], NN)
    mix1 = dot(key_weight, xv[TOK:, :], NN)
    row64 = lax.broadcasted_iota(jnp.int32, (8 * N_CAM, D), 0)
    mixture = jnp.where(lax.rem(row64, 8) >= PAIR, mix1, mix0).astype(BF16)
    head_out = dot(mixture, wv[...], NN)
    lane8 = lax.broadcasted_iota(jnp.int32, (8, LANES), 1)
    sub8 = lax.broadcasted_iota(jnp.int32, (8, LANES), 0)
    own_head = lax.rem(sub8, PAIR) == lax.div(lane8, HD)
    for p in range(N_CAM):
        tile = head_out[p * 8 : (p + 1) * 8, p * LANES : (p + 1) * LANES]
        tile = jnp.where(own_head, tile, 0.0)
        pool_send[p : p + 1, :] = tile[0:1] + tile[1:2]
        pool_send[N_CAM + p : N_CAM + p + 1, :] = tile[2:3] + tile[3:4]
    pool_out.start()
    pool_recv[cam] = pool_send[...]
    mixture_f = mixture.astype(F32)
    for p in range(N_CAM):
        mix_send[p] = mixture_f[p * 8 : p * 8 + PAIR * PAIR, :]
    mix_out.start()
    mix_recv[cam] = mix_send[cam]
    loads[6].wait()
    pool_out.landed()
    pooled = jnp.sum(pool_recv[...], axis=0).astype(BF16)
    row16 = lax.broadcasted_iota(jnp.int32, (PAIR * N_CAM, LANES), 0)
    spread = jnp.concatenate(
        [jnp.where(lax.rem(row16, N_CAM) == p, pooled, jnp.zeros_like(pooled)) for p in range(N_CAM)], axis=1
    )
    z_rows = dot(spread, wp[...], NN)
    for b in range(PAIR):
        z_clip = jnp.sum(z_rows[b * N_CAM : (b + 1) * N_CAM], axis=0, keepdims=True)
        for j in range(2):
            z_send[2 * b + j : 2 * b + j + 1, :] = z_clip[:, j * LANES : (j + 1) * LANES]
    pl.semaphore_wait(y_sem, N_Y - 1)
    z_out.start()
    z_recv[clip] = z_send[...]

    def left(b):
        for o in CAM_ORDER:
            k_copy(b, o).wait_send()

        def part_left(part):
            for o in CAM_ORDER:
                q_copy(b, part, o).wait_send()

        loop(0, PIECES, part_left)

    loop(0, PAIR, left)
    for i in range(N_Z - 1):
        proto_copy(i).wait_send()
    w_out.left()
    pool_out.left()

    mix_out.landed()
    mix_sum = jnp.sum(mix_recv[...], axis=0)
    pooled_f = pooled.astype(F32)
    for p in range(N_CAM):
        side_send[p, 0:1, :] = pooled_f[p : p + 1]
        side_send[p, 1:2, :] = pooled_f[N_CAM + p : N_CAM + p + 1]
        side_send[p, 2:6, :] = mix_sum[:, p * LANES : (p + 1) * LANES]
        side_send[p, 6:8, :] = jnp.zeros((2, LANES), F32)
    for i in range(N_Z - 1):
        proto_copy(i).wait_recv()
    z_out.landed()

    embed = jnp.concatenate(
        [jnp.concatenate([z_recv[:, 2 * b + j, :] for j in range(2)], axis=1) for b in range(PAIR)], axis=0
    )
    norm = jnp.sqrt(jnp.sum(embed * embed, axis=1, keepdims=True) + NORM_EPS)
    unit = embed / norm
    unit_buf[...] = unit
    norm_buf[...] = jnp.broadcast_to(norm, norm_buf.shape)
    unit_b = unit.astype(BF16)

    def total(step, sums, meanwhile=None):
        tall = jnp.broadcast_to(jnp.sum(sums, axis=1, keepdims=True), (LANES, LANES))
        row_send[step] = tall.T[:1, :]
        row_out[step].start()
        row_recv[step, here] = row_send[step]
        if meanwhile is not None:
            meanwhile()
        row_out[step].landed()
        wide = jnp.sum(row_recv[step], axis=0)
        return jnp.broadcast_to(wide, (LANES, LANES)).T

    zero = jnp.zeros((CLIPS, LANES), F32)

    def first(s, carry):
        rows, probs = carry
        exps = jnp.exp(dot(unit_b, proto_all[s], NN) * (1.0 / SOFTMAX_TEMP))
        scores = exps * exps
        p_buf[s] = exps
        a_buf[s] = scores
        scaled = scores * (1.0 / jnp.sum(scores, axis=0, keepdims=True))
        return rows + fold(scaled), probs + fold(exps)

    rows, probs = lax.fori_loop(0, N_Z, first, (zero, zero), unroll=True)

    def spread_rows(send, out, recv, value):
        for p in range(N_CAM):
            send[p] = value[p * 8 : (p + 1) * 8]
        out.start()
        recv[here] = send[cam]

    empty = jnp.zeros((CLIPS, BOT), F32)

    def while_waiting():
        side_out.start()
        side_recv[clip] = side_send[lax.div(clip * SHARE, LANES)]
        soft = lax.fori_loop(0, N_Z, lambda s, sums: sums + split_dot(p_buf[s], proto_all[s]), empty, unroll=True)
        spread_rows(gs_send, gs_out, gs_recv, soft)

    got = total(0, jnp.concatenate([rows, probs], axis=0), while_waiting)
    row_scale = 1.0 / got[:CLIPS]
    prob_scale = 1.0 / got[CLIPS:]
    prob_buf[...] = prob_scale

    def rescale(s, wide_scale):
        scores = a_buf[s]
        return scores * (1.0 / jnp.sum(scores * wide_scale, axis=0, keepdims=True))

    wide_scale = twice(row_scale)
    rows = lax.fori_loop(0, N_Z, lambda s, sums: sums + fold(rescale(s, wide_scale)), zero, unroll=True)
    row_scale = 1.0 / total(1, jnp.concatenate([rows, rows], axis=0))[:CLIPS]
    last_scale = twice(row_scale)

    def last(s, carry):
        rows, sums = carry
        scaled = rescale(s, last_scale)
        a_buf[s] = scaled
        return rows + fold(scaled), sums + split_dot(scaled, proto_all[s])

    rows, hard = lax.fori_loop(0, N_Z, last, (zero, empty), unroll=True)
    spread_rows(gu_send, gu_out, gu_recv, hard)
    row_scale = 1.0 / total(2, jnp.concatenate([rows, rows], axis=0))[:CLIPS]
    scale_buf[...] = row_scale

    mine = pl.ds(pl.multiple_of(cam * 8, 8), 8)
    gs_out.landed()
    grad8 = jnp.sum(gs_recv[...], axis=0) * twice(prob_buf[mine, :])
    gu_out.landed()
    grad8 = PROTOS * (grad8 - jnp.sum(gu_recv[...], axis=0) * twice(scale_buf[mine, :]))
    unit8 = unit_buf[mine, :]
    grad8 = (grad8 - unit8 * jnp.sum(unit8 * grad8, axis=1, keepdims=True)) / norm_buf[mine, :]
    gz_send[...] = grad8.astype(BF16).astype(F32)
    gz_out.start()
    gz_recv[cam] = gz_send[...]

    assigned = a_buf[z] * twice(row_scale)
    codes_out[...] = PROTOS * assigned
    logit_grad = (PROTOS * (p_buf[z] * twice(prob_scale) - assigned)).astype(BF16)
    grad_proto = dot(unit_b, logit_grad, TN)
    proto = pr[...].astype(F32)
    col_norm = jnp.sqrt(jnp.sum(proto * proto, axis=0, keepdims=True) + NORM_EPS)
    unit_proto = proto / col_norm
    proto_out[...] = (
        grad_proto - unit_proto * jnp.sum(unit_proto * grad_proto, axis=0, keepdims=True)
    ) / col_norm

    side_out.landed()
    part = pl.ds(pl.multiple_of(lax.rem(clip * SHARE, LANES), SHARE), SHARE)

    def features(row):
        tall = jnp.concatenate([side_recv[:, row(b), :] for b in range(PAIR)], axis=0).T
        side_tmp[:, :CLIPS] = tall
        return side_tmp[part, :][:, :CLIPS]

    pooled_all = features(lambda b: b).astype(BF16)
    parts = []
    for head in range(PAIR):
        mix_all = features(lambda b: 2 + PAIR * b + head)
        high = mix_all.astype(BF16)
        parts += [high, (mix_all - high.astype(F32)).astype(BF16)]
    mix_parts = jnp.concatenate(parts, axis=0)

    gz_out.landed()
    grad_z = gz_recv[...].reshape(CLIPS, BOT).astype(BF16)
    proj_out[...] = dot(pooled_all, grad_z, NN)
    grad_pooled = dot(grad_z, wp[pl.ds(pl.multiple_of(cam * LANES, LANES), LANES), :], NT).astype(BF16)
    by_head = dot(mix_parts, grad_pooled, NN)
    lane = lax.broadcasted_iota(jnp.int32, (SHARE, LANES), 1)
    value_out[...] = jnp.where(
        lane < HD,
        by_head[:SHARE] + by_head[SHARE : 2 * SHARE],
        by_head[2 * SHARE : 3 * SHARE] + by_head[3 * SHARE :],
    )

    for out in [mix_out, gz_out, z_out, side_out, gs_out, gu_out] + row_out:
        out.left()


def finish(codes, proto_grad, proj_grad, value_grad, codes_out, proto_out, proj_out, value_out, order):
    for j in range(COLS // LANES):
        columns = slice(j * LANES, (j + 1) * LANES)
        for b in range(PAIR):
            order[j, pl.ds(b, N_CLIP, stride=PAIR), :] = codes[b * N_CLIP : (b + 1) * N_CLIP, columns]
        codes_out[:, columns] = order[j]
    proto_out[...] = proto_grad[...]
    proj_out[...] = proj_grad[...]
    value_out[...] = value_grad[...]


def local(tokens, w_query, w_key, w_value, w_proj, prototypes):
    vmem, dma = pltpu.VMEM, pltpu.SemaphoreType.DMA
    shapes = (
        jax.ShapeDtypeStruct((CLIPS, COLS), F32),
        jax.ShapeDtypeStruct((BOT, COLS), F32),
        jax.ShapeDtypeStruct((SHARE, BOT), F32),
        jax.ShapeDtypeStruct((SHARE, LANES), F32),
    )
    got = pl.pallas_call(
        kernel,
        out_shape=shapes,
        in_specs=[pl.BlockSpec(memory_space=pl.ANY)] * 6,
        out_specs=[pl.BlockSpec(memory_space=pltpu.VMEM)] * 4,
        scratch_shapes=[
            vmem((PAIR * TOK, D), BF16), vmem((D, D), BF16), vmem((D, D), BF16), vmem((D, D), BF16),
            vmem((D, BOT), BF16), vmem((BOT, COLS), BF16),
            vmem((N_Z, BOT, COLS), BF16),
            vmem((PAIR, N_CAM, TOK, LANES), BF16), vmem((PAIR, N_CAM, TOK, LANES), BF16),
            vmem((PAIR, N_CAM, PIECES, PIECE, LANES), BF16), vmem((PAIR, PIECES, N_CAM, PIECE, LANES), BF16),
            vmem((PAIR * PAIR, 8, KEYS), F32),
            vmem((N_CAM, 8, TOK), F32), vmem((N_CAM, 8, TOK), F32),
            vmem((N_CAM, PAIR * PAIR, D), F32), vmem((N_CAM, PAIR * PAIR, D), F32),
            vmem((PAIR * N_CAM, LANES), F32), vmem((N_CAM, PAIR * N_CAM, LANES), F32),
            vmem((4, LANES), F32), vmem((N_CLIP, 4, LANES), F32),
            vmem((N_CAM, 8, LANES), F32), vmem((N_CLIP, 8, LANES), F32),
            vmem((N_Z, CLIPS, COLS), F32), vmem((N_Z, CLIPS, COLS), F32),
            vmem((CLIPS, BOT), F32), vmem((CLIPS, BOT), F32), vmem((CLIPS, LANES), F32), vmem((CLIPS, LANES), F32),
            vmem((3, 1, LANES), F32), vmem((3, N_R, 1, LANES), F32),
            vmem((N_CAM, 8, BOT), F32), vmem((N_R, 8, BOT), F32),
            vmem((N_CAM, 8, BOT), F32), vmem((N_R, 8, BOT), F32),
            vmem((8, BOT), F32), vmem((N_CAM, 8, BOT), F32),
            vmem((LANES, LANES), F32),
            dma((7,)), dma((PAIR, PIECES + 1)), pltpu.SemaphoreType.REGULAR,
            dma((PAIR, PIECES + 1, N_CAM)), dma((PAIR, PIECES + 1, N_CAM)), dma((4,)), dma((4,)),
            dma((N_Z,)), dma((N_Z,)), dma((7,)), dma((7,)),
        ],
        compiler_params=pltpu.CompilerParams(
            collective_id=0, has_side_effects=True, vmem_limit_bytes=VMEM_LIMIT
        ),
    )(tokens.reshape(PAIR * TOK, D), w_query, w_key, w_value, w_proj, prototypes)
    return pl.pallas_call(
        finish,
        out_shape=shapes,
        in_specs=[pl.BlockSpec(memory_space=pltpu.VMEM)] * 4,
        out_specs=[pl.BlockSpec(memory_space=pltpu.VMEM)] * 4,
        scratch_shapes=[vmem((COLS // LANES, CLIPS, LANES), F32)],
    )(*got)


def solution(mesh):
    assert mesh.shape["cam"] == N_CAM and mesh.shape["clip"] == N_CLIP
    in_specs = (P("clip", "cam", None, None), P(), P(), P(), P(), P(None, ("cam", "clip")))
    out_specs = (
        P(None, ("cam", "clip")),
        P(None, ("cam", "clip")),
        P("clip", None),
        P("clip", "cam"),
    )
    return jax.shard_map(local, mesh=mesh, in_specs=in_specs, out_specs=out_specs, check_vma=False)
```
